256 devices in a mesh: tm: 64 (over y, z, core), col: 4 (over x).
Axes of the slice: x: 4, y: 4, z: 8, core: 2. Of those that a mesh axis runs over, the one named last changes fastest.
Arguments:
- transition: bfloat16 [512, 256, 256], P('tm', 'col'), may hold values from -1 to 1, as said below
- drive: float32 [512, 16, 256], P('tm', 'col'), may hold values from -0.3125 to 0.3125
- smoother_gain: bfloat16 [512, 256, 256], P('tm', 'col'), may hold values from -1 to 1, as said below
- dynamics: float32 [256, 256], replicated, may hold values from -0.375 to 0.375
- initial_mean: float32 [16, 256], P('col'), may hold values from -6 to 6
Outputs:
- filtered_mean: float32 [512, 16, 256], P('tm', 'col')
- smoothed_mean: float32 [512, 16, 256], P('tm', 'col')
The draws below stay inside these ranges and needn't reach their ends.
Inputs may be any that keep to these rules, and one draw needn't show every extreme that they name: `transition`: every step operator is a per-channel diagonal plus a dense full-rank part. `smoother_gain`: every gain is a per-channel diagonal plus a dense full-rank part.
All inputs are finite; a program needn't handle non-finite values.
Results may differ from the reference program's by a relative error of at most 0.0018.
Values may be sent and summed in bfloat16 or wider, within the bound.
No kernel may reach another device: no remote copies, remote signals or barrier semaphores. Data moves between devices by JAX's collectives and lax.ppermute only.
A program may use at most 128 MiB of HBM per device.

```python
import jax
import jax.numpy as jnp
from jax import lax

D = 256
TIME_STEP_COUNT = 512
SERIES = 16


def operator_draw(key, salt):
    baseline_level = jax.random.fold_in(key, salt)
    arrival_rate_key, jitter_noise_key, spike_event_key = jax.random.split(baseline_level, 3)
    rates = 0.85 + 0.14 * jax.random.uniform(arrival_rate_key, (D,), jnp.float32)
    noise = jax.random.normal(jitter_noise_key, (TIME_STEP_COUNT, D, D), jnp.float32)
    spike_events = jax.random.randint(spike_event_key, (4,), 0, TIME_STEP_COUNT)
    step_values = jnp.arange(TIME_STEP_COUNT)
    spike_hits = jnp.any(step_values[:, None] == spike_events[None, :], axis=1)
    diagonal = rates[None, :] * jnp.where(spike_hits, 0.6, 1.0)[:, None]
    ident = jnp.eye(D, dtype=jnp.float32)
    result = noise * (0.39 * D ** (-0.5)) + ident[None, :, :] * diagonal[:, None, :]
    return jnp.clip(result, -1.0, 1.0)


def draw_transition(key, part):
    return operator_draw(key, 11).astype(jnp.bfloat16)


def draw_smoother_gain(key, part):
    return operator_draw(key, 23).astype(jnp.bfloat16)


def shard_levels(key, dims, pieces, low, high):
    def one(dim, parts):
        draws = jax.random.uniform(jax.random.fold_in(jax.random.fold_in(key, 6), dim), (parts,), jnp.float32, low / len(pieces), high / len(pieces))
        return jnp.repeat(jnp.exp(draws), dims[dim] // parts).reshape((-1,) + (1,) * (len(dims) - dim - 1))

    level = one(*pieces[0])
    for cut in pieces[1:]:
        level = level * one(*cut)
    return level


def scatter_about(key, dims, scale, reach, cuts=(), held_as=jnp.bfloat16):
    drawn = scale * jax.random.normal(key, dims, jnp.float32)
    if cuts:
        drawn = drawn * shard_levels(key, dims, cuts, -0.22, 0.18)
    return jnp.clip(drawn, -reach, reach).astype(held_as)


def setup_inputs(seed: int = 0) -> dict:
    streams_of = jax.random.split(jax.random.key(seed), 6)
    return {
        "transition": draw_transition(jax.random.fold_in(streams_of[5], 71), 0),
        "drive": scatter_about(streams_of[1], (TIME_STEP_COUNT, SERIES, D), 0.05, 0.3125, ((0, 64), (1, 4)), jnp.float32),
        "smoother_gain": draw_smoother_gain(jax.random.fold_in(streams_of[5], 71), 0),
        "dynamics": scatter_about(streams_of[3], (D, D), D ** -0.5, 0.375, (), jnp.float32),
        "initial_mean": scatter_about(streams_of[4], (SERIES, D), 1.0, 6.0, ((0, 4),), jnp.float32),
    }


highest = lax.Precision.HIGHEST


def reference(transition, drive, smoother_gain, dynamics, initial_mean):
    positions = jnp.arange(TIME_STEP_COUNT)
    keep = positions < TIME_STEP_COUNT - 1
    gains = jnp.where(keep[:, None, None], smoother_gain, jnp.zeros_like(smoother_gain))

    def forward_step(state, inputs):
        operator, push = inputs
        state = jnp.dot(state, operator.astype(jnp.float32), precision=highest, preferred_element_type=jnp.float32) + push
        return state, state

    _, filtered = lax.scan(forward_step, initial_mean.astype(jnp.float32), (transition, drive))

    def correct_step(carry, inputs):
        mean_now, gain_now = inputs
        projected = jnp.dot(mean_now, dynamics, precision=highest, preferred_element_type=jnp.float32)
        result = mean_now - jnp.dot(projected, gain_now.astype(jnp.float32), precision=highest, preferred_element_type=jnp.float32)
        return carry, result

    _, correction = lax.scan(correct_step, jnp.float32(0.0), (filtered, gains))

    def backward_step(state, inputs):
        gain_now, corr_now = inputs
        state = jnp.dot(state, gain_now.astype(jnp.float32), precision=highest, preferred_element_type=jnp.float32) + corr_now
        return state, state

    begin = jnp.zeros((SERIES, D), jnp.float32)
    _, smoothed = lax.scan(backward_step, begin, (gains, correction), reverse=True)
    return filtered, smoothed
```

```python
import jax
import jax.numpy as jnp
from jax import lax
from jax.experimental import pallas as pl
from jax.experimental.pallas import tpu as pltpu
from jax.sharding import PartitionSpec as P

F_COLS, S_COLS = (0, 3), (1, 2)
PARTNER = {0: 1, 3: 2}
D = 256
SER = 8
ROWS = D // 2 + SER
f32, bf16 = jnp.float32, jnp.bfloat16


def split(x):
    hi = x.astype(bf16)
    return hi, (x - hi.astype(f32)).astype(bf16)


def dot(a, b):
    return jnp.dot(a, b, preferred_element_type=f32)


def mul_exact(x, b):
    hi, lo = split(x)
    return dot(hi, b) + dot(lo, b)


def mul(x, b):
    hi, lo = split(x)
    bhi, blo = split(b)
    return dot(hi, bhi) + (dot(lo, bhi) + dot(hi, blo))


def is_f(col):
    return jnp.logical_or(col == 0, col == 3)


def assemble(dst, pieces, col):
    rows = pieces[0].shape[1]
    for lag, piece in enumerate(pieces):
        at = pl.multiple_of(lax.rem(col - lag + 4, 4) * rows, rows)
        dst[:, pl.ds(at, rows), :] = piece[...]


def block_kernel(a0, a1, a2, a3, g0, drive, mean, raw, out):
    tm, col = lax.axis_index("tm"), lax.axis_index("col")
    forward = is_f(col)
    steps = a0.shape[0]
    assemble(raw, (a0, a1, a2, a3), col)

    @pl.when(jnp.logical_not(forward))
    def _():
        rows = g0.shape[1]
        raw[:, pl.ds(pl.multiple_of(col * rows, rows), rows), :] = g0[...]

    @pl.when(jnp.logical_and(jnp.logical_not(forward), tm == lax.axis_size("tm") - 1))
    def _():
        raw[steps - 1] = jnp.zeros((D, D), bf16)

    scale = jnp.where(forward, 1.0, 0.0).astype(f32)
    first = jnp.where(forward, 0, steps - 1)
    start = jnp.where(jnp.logical_and(forward, tm == 0), 1.0, 0.0).astype(f32)
    out[:D, :] = raw[first].astype(f32)
    out[D:, :] = mul_exact(mean[...] * start, raw[first]) + drive[0] * scale

    def step(i, carry):
        t = jnp.where(forward, i, steps - 1 - i)
        new = mul_exact(out[...], raw[t])
        out[:D, :] = new[:D]
        out[D:, :] = new[D:] + drive[i] * scale
        return carry

    lax.fori_loop(1, steps, step, 0)


def pair_kernel(own, other, left, right, out):
    tm, col = lax.axis_index("tm"), lax.axis_index("col")
    core = lax.rem(tm, 2)
    forward = is_f(col)
    own_left = forward == (core == 0)
    left[...] = jnp.where(own_left, own[...], other[...])
    right[...] = jnp.where(own_left, other[...], own[...])
    at = pl.multiple_of(core * (D // 2), D // 2)
    r = right[:D, :]
    out[: D // 2, :] = mul(left[pl.ds(at, D // 2), :], r)
    out[D // 2 :, :] = mul(left[D:, :], r) + right[D:, :]


def join(dst, own, other, core):
    half = D // 2
    at = pl.multiple_of(core * half, half)
    dst[pl.ds(at, half), :] = own[:half, :]
    dst[pl.ds(pl.multiple_of(half - at, half), half), :] = other[:half, :]


def round_kernel(dist, own, other, got, out, full):
    tm, col = lax.axis_index("tm"), lax.axis_index("col")
    core = lax.rem(tm, 2)
    chip = lax.div(tm, 2)
    chips = lax.axis_size("tm") // 2
    join(full, own, other, core)
    forward = is_f(col)
    valid = jnp.where(forward, chip >= dist, chip + dist < chips)
    new = mul(got[...], full[...])
    half = D // 2
    out[:half, :] = jnp.where(valid, new[:half], own[:half, :])
    out[half:, :] = new[half:] + own[half:, :]


def vec_kernel(own, other, vec, got, out, full):
    join(full, own, other, lax.rem(lax.axis_index("tm"), 2))
    out[...] = mul(got[...], full[...]) + vec[...]


def mid_kernel(a0, a1, a2, a3, g, drive, mean, got, head, dyn, xs, cs, w, araw):
    tm, col = lax.axis_index("tm"), lax.axis_index("col")
    core = lax.rem(tm, 2)
    steps = g.shape[0]
    assemble(araw, (a0, a1, a2, a3), col)
    begin = got[...] + jnp.where(tm == 0, 1.0, 0.0).astype(f32) * mean[...]
    later = mul(begin, head[:D, :]) + head[D:, :]
    x = jnp.where(core == 0, begin, later)
    for t in range(steps):
        x = mul_exact(x, araw[t]) + drive[t]
        xs[t] = x
    flat = xs[...].reshape(steps * SER, D)
    proj = mul(flat, dyn[...])
    for t in range(steps):
        cs[t] = xs[t] - mul_exact(proj[t * SER : (t + 1) * SER], g[t])
    s = cs[steps - 1]
    for t in range(steps - 2, -1, -1):
        s = mul_exact(s, g[t]) + cs[t]
    w[...] = s


def chip_vec_kernel(w, w_other, right, out):
    core = lax.rem(lax.axis_index("tm"), 2)
    first = jnp.where(core == 0, w[...], w_other[...])
    second = jnp.where(core == 0, w_other[...], w[...])
    out[...] = mul(second, right[:D, :]) + first


def last_kernel(g, cs, w_other, got, left, ss):
    core = lax.rem(lax.axis_index("tm"), 2)
    steps = g.shape[0]
    mid = mul(got[...], left[:D, :]) + w_other[...]
    s = jnp.where(core == 0, mid, got[...])
    for t in range(steps - 1, -1, -1):
        s = mul_exact(s, g[t]) + cs[t]
        ss[t] = s


VM = pl.BlockSpec(memory_space=pltpu.VMEM)


def call(kernel, outs, scratch, *args):
    return pl.pallas_call(
        kernel,
        out_shape=tuple(jax.ShapeDtypeStruct(s, d) for s, d in outs),
        in_specs=[VM] * len(args),
        out_specs=tuple(VM for _ in outs),
        scratch_shapes=[pltpu.VMEM(s, d) for s, d in scratch],
    )(*args)


def local(transition, drive, smoother_gain, dynamics, initial_mean):
    tms, cols = lax.axis_size("tm"), lax.axis_size("col")
    steps = transition.shape[0]
    chips = tms // 2
    col = lax.axis_index("col")

    def both(pairs):
        return [(a * cols + b, c * cols + d) for (a, b), (c, d) in pairs]

    def send(x, pairs):
        return lax.ppermute(x, ("tm", "col"), both(pairs))

    def swap_core(x):
        return lax.ppermute(x, "tm", [(i, i ^ 1) for i in range(tms)])

    def shift(x, dist):
        pairs = []
        for chip in range(chips):
            for core in range(2):
                for c in range(cols):
                    to = chip + dist if c in F_COLS else chip - dist
                    if 0 <= to < chips:
                        pairs.append(((2 * chip + core, c), (2 * to + core, c)))
        return send(x, pairs)

    got = []
    for lag in (1, 2, 3):
        target_f = is_f(lax.rem(col + lag, 4))
        got.append(
            lax.ppermute(
                jnp.where(target_f, transition, smoother_gain),
                "col",
                [(c, (c + lag) % 4) for c in range(cols)],
            )
        )
    extra = jnp.concatenate([drive, initial_mean[None]], 0)
    swapped = lax.ppermute(extra, "col", [(0, 1), (1, 0), (2, 3), (3, 2)])
    odd = lax.rem(col, 2) == 1
    eight = jnp.where(
        odd, jnp.concatenate([swapped, extra], 1), jnp.concatenate([extra, swapped], 1)
    )
    drive8, mean8 = eight[:steps], eight[steps]

    raw, block = call(
        block_kernel,
        [((steps, D, D), bf16), ((D + SER, D), f32)],
        [],
        transition, got[0], got[1], got[2], smoother_gain, drive8, mean8,
    )
    other = swap_core(block)
    left, right, own = call(
        pair_kernel,
        [((D + SER, D), f32), ((D + SER, D), f32), ((ROWS, D), f32)],
        [],
        block, other,
    )
    head = send(
        left,
        [((2 * k + 1, f), (2 * k + 1, PARTNER[f])) for k in range(chips) for f in F_COLS],
    )
    agot = []
    for lag in (1, 2, 3):
        agot.append(
            lax.ppermute(
                transition, "col", [((s - lag) % 4, s) for s in S_COLS]
            )
        )

    levels = []
    for dist in (1, 2, 4, 8):
        mate = swap_core(own)
        levels.append((own, mate))
        recv = shift(own, dist)
        (own,) = call(
            lambda *r, dist=dist: round_kernel(dist, *r),
            [((ROWS, D), f32)],
            [((D, D), f32)],
            own, mate, recv,
        )
    mate = swap_core(own)
    levels.append((own, mate))
    vec = own[D // 2 :]
    recv = shift(vec, 16)
    (vec,) = call(
        vec_kernel, [((SER, D), f32)], [((D, D), f32)], own, mate, vec, recv
    )
    entering = send(
        vec,
        [
            ((2 * k + h, f), (2 * k + 2 + h, PARTNER[f]))
            for k in range(chips - 1)
            for h in range(2)
            for f in F_COLS
        ],
    )
    xs, cs, w = call(
        mid_kernel,
        [((steps, SER, D), f32), ((steps, SER, D), f32), ((SER, D), f32)],
        [((steps, D, D), bf16)],
        transition, agot[0], agot[1], agot[2], raw, drive8, mean8, entering, head, dynamics,
    )
    w_other = swap_core(w)
    (vec,) = call(chip_vec_kernel, [((SER, D), f32)], [], w, w_other, right)
    for level, dist in enumerate((1, 2, 4, 8, 16)):
        recv = shift(vec, dist)
        (vec,) = call(
            vec_kernel,
            [((SER, D), f32)],
            [((D, D), f32)],
            levels[level][0], levels[level][1], vec, recv,
        )
    entering = shift(vec, 1)
    (ss,) = call(
        last_kernel, [((steps, SER, D), f32)], [], raw, cs, w_other, entering, left
    )
    first = col < 2

    def place(y):
        low, high = y[:, :4], y[:, 4:]
        got = lax.ppermute(jnp.where(first, low, high), "col", [(1, 0), (2, 3)])
        keep = jnp.where(first, high, low)
        return jnp.where(is_f(col), got, keep)

    return place(xs), place(ss)


def solution(mesh):
    placed = (P("tm", "col", None), P("tm", "col", None), P("tm", "col", None), P(), P("col", None))
    return jax.shard_map(
        local,
        mesh=mesh,
        in_specs=placed,
        out_specs=(P("tm", "col", None), P("tm", "col", None)),
        check_vma=False,
    )
```

```python
import jax
import jax.numpy as jnp
from jax import lax
from jax.experimental import pallas as pl
from jax.experimental.pallas import tpu as pltpu
from jax.sharding import PartitionSpec as P

F_COLS, S_COLS = (0, 3), (1, 2)
PARTNER = {0: 1, 3: 2}
D = 256
SER = 8
ROWS = D // 2 + SER
VMEM_BYTES = 8 << 20
f32, bf16 = jnp.float32, jnp.bfloat16


def split(x):
    hi = x.astype(bf16)
    return hi, (x - hi.astype(f32)).astype(bf16)


def dot(a, b):
    return jnp.dot(a, b, preferred_element_type=f32)


def mul_exact(x, b):
    hi, lo = split(x)
    return dot(hi, b) + dot(lo, b)


def mul(x, b):
    hi, lo = split(x)
    bhi, blo = split(b)
    return dot(hi, bhi) + (dot(lo, bhi) + dot(hi, blo))


def is_f(col):
    return jnp.logical_or(col == 0, col == 3)


def assemble(dst, pieces, col):
    rows = pieces[0].shape[1]
    for lag, piece in enumerate(pieces):
        at = pl.multiple_of(lax.rem(col - lag + 4, 4) * rows, rows)
        dst[:, pl.ds(at, rows), :] = piece[...]


def block_kernel(a0, a1, a2, a3, g0, drive, mean, raw, out):
    tm, col = lax.axis_index("tm"), lax.axis_index("col")
    forward = is_f(col)
    steps = a0.shape[0]
    assemble(raw, (a0, a1, a2, a3), col)

    @pl.when(jnp.logical_not(forward))
    def _():
        rows = g0.shape[1]
        raw[:, pl.ds(pl.multiple_of(col * rows, rows), rows), :] = g0[...]

    @pl.when(jnp.logical_and(jnp.logical_not(forward), tm == lax.axis_size("tm") - 1))
    def _():
        raw[steps - 1] = jnp.zeros((D, D), bf16)

    scale = jnp.where(forward, 1.0, 0.0).astype(f32)
    first = jnp.where(forward, 0, steps - 1)
    start = jnp.where(jnp.logical_and(forward, tm == 0), 1.0, 0.0).astype(f32)
    out[:D, :] = raw[first].astype(f32)
    out[D:, :] = mul_exact(mean[...] * start, raw[first]) + drive[0] * scale

    def step(i, carry):
        t = jnp.where(forward, i, steps - 1 - i)
        new = mul_exact(out[...], raw[t])
        out[:D, :] = new[:D]
        out[D:, :] = new[D:] + drive[i] * scale
        return carry

    lax.fori_loop(1, steps, step, 0)


def pair_kernel(own, other, left, right, out):
    tm, col = lax.axis_index("tm"), lax.axis_index("col")
    core = lax.rem(tm, 2)
    forward = is_f(col)
    own_left = forward == (core == 0)
    left[...] = jnp.where(own_left, own[...], other[...])
    right[...] = jnp.where(own_left, other[...], own[...])
    at = pl.multiple_of(core * (D // 2), D // 2)
    r = right[:D, :]
    out[: D // 2, :] = mul(left[pl.ds(at, D // 2), :], r)
    out[D // 2 :, :] = mul(left[D:, :], r) + right[D:, :]


def join(dst, own, other, core):
    half = D // 2
    at = pl.multiple_of(core * half, half)
    dst[pl.ds(at, half), :] = own[:half, :]
    dst[pl.ds(pl.multiple_of(half - at, half), half), :] = other[:half, :]


def round_kernel(dist, own, other, got, out, full):
    tm, col = lax.axis_index("tm"), lax.axis_index("col")
    core = lax.rem(tm, 2)
    chip = lax.div(tm, 2)
    chips = lax.axis_size("tm") // 2
    join(full, own, other, core)
    forward = is_f(col)
    valid = jnp.where(forward, chip >= dist, chip + dist < chips)
    new = mul(got[...], full[...])
    half = D // 2
    out[:half, :] = jnp.where(valid, new[:half], own[:half, :])
    out[half:, :] = new[half:] + own[half:, :]


def vec_kernel(own, other, vec, got, out, full):
    join(full, own, other, lax.rem(lax.axis_index("tm"), 2))
    out[...] = mul(got[...], full[...]) + vec[...]


def mid_kernel(a0, a1, a2, a3, g, drive, mean, got, head, dyn, xs, cs, w, araw):
    tm, col = lax.axis_index("tm"), lax.axis_index("col")
    core = lax.rem(tm, 2)
    steps = g.shape[0]
    assemble(araw, (a0, a1, a2, a3), col)
    begin = got[...] + jnp.where(tm == 0, 1.0, 0.0).astype(f32) * mean[...]
    later = mul(begin, head[:D, :]) + head[D:, :]
    x = jnp.where(core == 0, begin, later)
    for t in range(steps):
        x = mul_exact(x, araw[t]) + drive[t]
        xs[t] = x
    flat = xs[...].reshape(steps * SER, D)
    proj = mul(flat, dyn[...])
    for t in range(steps):
        cs[t] = xs[t] - mul_exact(proj[t * SER : (t + 1) * SER], g[t])
    s = cs[steps - 1]
    for t in range(steps - 2, -1, -1):
        s = mul_exact(s, g[t]) + cs[t]
    w[...] = s


def chip_vec_kernel(w, w_other, right, out):
    core = lax.rem(lax.axis_index("tm"), 2)
    first = jnp.where(core == 0, w[...], w_other[...])
    second = jnp.where(core == 0, w_other[...], w[...])
    out[...] = mul(second, right[:D, :]) + first


def last_kernel(g, cs, w_other, got, left, ss):
    core = lax.rem(lax.axis_index("tm"), 2)
    steps = g.shape[0]
    mid = mul(got[...], left[:D, :]) + w_other[...]
    s = jnp.where(core == 0, mid, got[...])
    for t in range(steps - 1, -1, -1):
        s = mul_exact(s, g[t]) + cs[t]
        ss[t] = s


VM = pl.BlockSpec(memory_space=pltpu.VMEM)


def call(kernel, outs, scratch, *args):
    return pl.pallas_call(
        kernel,
        out_shape=tuple(jax.ShapeDtypeStruct(s, d) for s, d in outs),
        in_specs=[VM] * len(args),
        out_specs=tuple(VM for _ in outs),
        scratch_shapes=[pltpu.VMEM(s, d) for s, d in scratch],
        compiler_params=pltpu.CompilerParams(vmem_limit_bytes=VMEM_BYTES),
    )(*args)


def local(transition, drive, smoother_gain, dynamics, initial_mean):
    tms, cols = lax.axis_size("tm"), lax.axis_size("col")
    steps = transition.shape[0]
    chips = tms // 2
    col = lax.axis_index("col")

    def both(pairs):
        return [(a * cols + b, c * cols + d) for (a, b), (c, d) in pairs]

    def send(x, pairs):
        return lax.ppermute(x, ("tm", "col"), both(pairs))

    def swap_core(x):
        return lax.ppermute(x, "tm", [(i, i ^ 1) for i in range(tms)])

    def shift(x, dist):
        pairs = []
        for chip in range(chips):
            for core in range(2):
                for c in range(cols):
                    to = chip + dist if c in F_COLS else chip - dist
                    if 0 <= to < chips:
                        pairs.append(((2 * chip + core, c), (2 * to + core, c)))
        return send(x, pairs)

    got = []
    for lag in (1, 2, 3):
        target_f = is_f(lax.rem(col + lag, 4))
        got.append(
            lax.ppermute(
                jnp.where(target_f, transition, smoother_gain),
                "col",
                [(c, (c + lag) % 4) for c in range(cols)],
            )
        )
    extra = jnp.concatenate([drive, initial_mean[None]], 0)
    swapped = lax.ppermute(extra, "col", [(0, 1), (1, 0), (2, 3), (3, 2)])
    odd = lax.rem(col, 2) == 1
    eight = jnp.where(
        odd, jnp.concatenate([swapped, extra], 1), jnp.concatenate([extra, swapped], 1)
    )
    drive8, mean8 = eight[:steps], eight[steps]

    raw, block = call(
        block_kernel,
        [((steps, D, D), bf16), ((D + SER, D), f32)],
        [],
        transition, got[0], got[1], got[2], smoother_gain, drive8, mean8,
    )
    other = swap_core(block)
    left, right, own = call(
        pair_kernel,
        [((D + SER, D), f32), ((D + SER, D), f32), ((ROWS, D), f32)],
        [],
        block, other,
    )
    head = send(
        left,
        [((2 * k + 1, f), (2 * k + 1, PARTNER[f])) for k in range(chips) for f in F_COLS],
    )
    agot = []
    for lag in (1, 2, 3):
        agot.append(
            lax.ppermute(
                transition, "col", [((s - lag) % 4, s) for s in S_COLS]
            )
        )

    levels = []
    for dist in (1, 2, 4, 8):
        mate = swap_core(own)
        levels.append((own, mate))
        recv = shift(own, dist)
        (own,) = call(
            lambda *r, dist=dist: round_kernel(dist, *r),
            [((ROWS, D), f32)],
            [((D, D), f32)],
            own, mate, recv,
        )
    mate = swap_core(own)
    levels.append((own, mate))
    vec = own[D // 2 :]
    recv = shift(vec, 16)
    (vec,) = call(
        vec_kernel, [((SER, D), f32)], [((D, D), f32)], own, mate, vec, recv
    )
    entering = send(
        vec,
        [
            ((2 * k + h, f), (2 * k + 2 + h, PARTNER[f]))
            for k in range(chips - 1)
            for h in range(2)
            for f in F_COLS
        ],
    )
    xs, cs, w = call(
        mid_kernel,
        [((steps, SER, D), f32), ((steps, SER, D), f32), ((SER, D), f32)],
        [((steps, D, D), bf16)],
        transition, agot[0], agot[1], agot[2], raw, drive8, mean8, entering, head, dynamics,
    )
    w_other = swap_core(w)
    (vec,) = call(chip_vec_kernel, [((SER, D), f32)], [], w, w_other, right)
    for level, dist in enumerate((1, 2, 4, 8, 16)):
        recv = shift(vec, dist)
        (vec,) = call(
            vec_kernel,
            [((SER, D), f32)],
            [((D, D), f32)],
            levels[level][0], levels[level][1], vec, recv,
        )
    entering = shift(vec, 1)
    (ss,) = call(
        last_kernel, [((steps, SER, D), f32)], [], raw, cs, w_other, entering, left
    )
    first = col < 2

    def place(y):
        low, high = y[:, :4], y[:, 4:]
        got = lax.ppermute(jnp.where(first, low, high), "col", [(1, 0), (2, 3)])
        keep = jnp.where(first, high, low)
        return jnp.where(is_f(col), got, keep)

    return place(xs), place(ss)


def solution(mesh):
    placed = (P("tm", "col", None), P("tm", "col", None), P("tm", "col", None), P(), P("col", None))
    return jax.shard_map(
        local,
        mesh=mesh,
        in_specs=placed,
        out_specs=(P("tm", "col", None), P("tm", "col", None)),
        check_vma=False,
    )
```

```python
import jax
import jax.numpy as jnp
from jax import lax
from jax.experimental import pallas as pl
from jax.experimental.pallas import tpu as pltpu
from jax.sharding import PartitionSpec as P

SUF_X, SUF_Y, SUF_Q, PRE_X = 0, 1, 2, 3
D = 256
HALF = D // 2
SER = 16
GRP = 8
ALL = D + SER
ROWS = HALF + GRP
f32, bf16 = jnp.float32, jnp.bfloat16


def split(x):
    hi = x.astype(bf16)
    return hi, (x - hi.astype(f32)).astype(bf16)


def dot(a, b):
    return jnp.dot(a, b, preferred_element_type=f32)


def mul_exact(x, b):
    hi, lo = split(x)
    return dot(hi, b) + dot(lo, b)


def mul(x, b):
    hi, lo = split(x)
    bhi, blo = split(b)
    return dot(hi, bhi) + (dot(lo, bhi) + dot(hi, blo))


def place():
    tm = lax.axis_index("tm")
    return tm, lax.rem(tm, 2), lax.axis_index("col")


def aligned(index, unit):
    return pl.multiple_of(index * unit, unit)


def assemble(dst, pieces, col):
    rows = pieces[0].shape[1]
    for lag, piece in zip((0, 3, 1, 2), pieces):
        dst[:, pl.ds(aligned(lax.rem(col + lag, 4), rows), rows), :] = piece[...]


def forward_kernel(
    a0, a1, a2, a3, g0, g1, g2, g3, d0, d1, d2, d3, araw, graw, drive, xs, x_out, q_out
):
    tm, core, col = place()
    steps = a0.shape[0]
    assemble(araw, (a0, a1, a2, a3), col)
    assemble(graw, (g0, g1, g2, g3), col)
    per = d0.shape[1]
    for c in range(4):

        @pl.when(col == c)
        def _(c=c):
            for lag, piece in zip((0, 3, 1, 2), (d0, d1, d2, d3)):
                at = (c + lag) % 4 * per
                drive[:, at : at + per, :] = piece[...]

    @pl.when(tm == lax.axis_size("tm") - 1)
    def _():
        graw[steps - 1] = jnp.zeros((D, D), bf16)

    start = jnp.where(tm == 0, 1.0, 0.0).astype(f32)
    xs[0, :D, :] = araw[0].astype(f32)
    xs[0, D:, :] = mul_exact(drive[steps] * start, araw[0]) + drive[0]
    q = graw[steps - 1].astype(f32)
    for t in range(1, steps):
        new = mul_exact(xs[t - 1], araw[t])
        q = mul_exact(q, graw[steps - 1 - t])
        xs[t, :D, :] = new[:D]
        xs[t, D:, :] = new[D:] + drive[t]
    x_out[...] = xs[steps - 1]
    q_out[...] = q


def backward_kernel(xs, graw, dyn, y_out):
    steps = xs.shape[0]
    dhi, dlo = split(dyn[...])
    s = None
    for t in range(steps - 1, -1, -1):
        x = xs[t]
        hi, lo = split(x)
        proj = dot(hi, dhi) + (dot(lo, dhi) + dot(hi, dlo))
        s = mul_exact(-proj if s is None else s - proj, graw[t]) + x
    y_out[...] = s


def rows_of(ref, core):
    return jnp.concatenate(
        [ref[pl.ds(aligned(core, HALF), HALF), :], ref[pl.ds(aligned(core, GRP) + D, GRP), :]], 0
    )


def chip_kernel(x, x_m, q, q_m, y, y_m, own, xrow, qrow, qrow_m):
    tm, core, col = place()

    def work(x0, q0, y0, x1, q1, y1):
        zero = jnp.zeros((HALF, D), f32)
        left = rows_of(x0, core)
        series = pl.ds(aligned(core, GRP) + D, GRP)
        new_x = mul(left, x1[:D, :]) + jnp.concatenate([zero, x1[series, :]], 0)
        xrow[...] = new_x
        q_left = q0[...]
        new_q = mul(q1[pl.ds(aligned(core, HALF), HALF), :], q_left)
        qrow[:HALF, :] = new_q
        qrow[HALF:, :] = jnp.zeros((GRP, D), f32)
        qrow_m[:HALF, :] = mul(q1[pl.ds(aligned(1 - core, HALF), HALF), :], q_left)
        qrow_m[HALF:, :] = jnp.zeros((GRP, D), f32)
        mid = mul(left, y1[:D, :]) + jnp.concatenate([zero, y1[series, :]], 0)
        new_y = rows_of(y0, core) + mul(mid, q_left)
        own[...] = jnp.where(col == SUF_Y, new_y, jnp.where(col == SUF_Q, qrow[...], new_x))

    @pl.when(core == 0)
    def _():
        work(x, q, y, x_m, q_m, y_m)

    @pl.when(core == 1)
    def _():
        work(x_m, q_m, y_m, x, q, y)


def join(dst, own, mate, core):
    dst[pl.ds(aligned(core, HALF), HALF), :] = own[:HALF, :]
    dst[pl.ds(aligned(1 - core, HALF), HALF), :] = mate[:HALF, :]


def round_kernel(dist, own, own_m, got, got_m, xrow, qrow, qrow_m, out, full):
    tm, core, col = place()
    chip = lax.div(tm, 2)
    chips = lax.axis_size("tm") // 2

    @pl.when(jnp.logical_or(col == PRE_X, col == SUF_Q))
    def _():
        join(full, own, own_m, core)
        valid = jnp.where(col == PRE_X, chip >= dist, chip + dist < chips)
        new = mul(got[...], full[...])
        out[:HALF, :] = jnp.where(valid, new[:HALF], own[:HALF, :])
        out[HALF:, :] = new[HALF:] + own[HALF:, :]

    @pl.when(col == SUF_X)
    def _():
        join(full, got, got_m, core)
        new = mul(own[...], full[...])
        valid = chip + dist < chips
        out[:HALF, :] = jnp.where(valid, new[:HALF], own[:HALF, :])
        out[HALF:, :] = jnp.where(valid, new[HALF:] + got[HALF:, :], own[HALF:, :])

    @pl.when(col == SUF_Y)
    def _():
        join(full, got, got_m, core)
        mid = mul(xrow[...], full[...])
        mid = jnp.concatenate([mid[:HALF], mid[HALF:] + got[HALF:, :]], 0)
        join(full, qrow, qrow_m, core)
        out[...] = own[...] + mul(mid, full[...])


def mean_kernel(own, own_m, got, out, full):
    tm, core, col = place()
    join(full, own, own_m, core)
    out[...] = mul(got[...], full[...]) + own[HALF:, :]


def series_of(own, mate, core):
    first = jnp.where(core == 0, own, mate)
    second = jnp.where(core == 0, mate, own)
    return jnp.concatenate([first, second], 0)


def top_kernel(
    own, own_m, xrow, xrow_m, qrow, qrow_m, got, got_m, x, x_m, s_lo, s_hi, x_lo, x_hi, full
):
    tm, core, col = place()
    begin = series_of(x[...], x_m[...], core)
    join(full, own, own_m, core)
    s = mul(begin, full[...]) + series_of(own[HALF:, :], own_m[HALF:, :], core)
    join(full, xrow, xrow_m, core)
    mid = mul(begin, full[...]) + series_of(xrow[HALF:, :], xrow_m[HALF:, :], core)
    join(full, got, got_m, core)
    far = mul(mid, full[...]) + series_of(got[HALF:, :], got_m[HALF:, :], core)
    join(full, qrow, qrow_m, core)
    s = s + mul(far, full[...])
    s_lo[...] = s[:GRP]
    s_hi[...] = s[GRP:]
    x_lo[...] = begin[:GRP]
    x_hi[...] = begin[GRP:]


def mean_sweep_kernel(araw, drive, dyn, x_b, x_bm, x_r, x0, x2, x3, xs, proj, mid, filt):
    tm, core, col = place()
    steps = araw.shape[0]
    low = col < 2
    begin = jnp.where(col == SUF_Y, x_r[...], x0[...] + x2[...] + x3[...])

    def group(ref):
        return jnp.where(low, ref[D : D + GRP, :], ref[D + GRP :, :])

    @pl.when(core == 0)
    def _():
        mid[...] = mul(begin, x_b[:D, :]) + group(x_b)

    @pl.when(core == 1)
    def _():
        mid[...] = mul(begin, x_bm[:D, :]) + group(x_bm)

    mean = jnp.where(low, drive[steps, :GRP, :], drive[steps, GRP:, :])
    first = begin + jnp.where(tm == 0, 1.0, 0.0).astype(f32) * mean
    x = jnp.where(core == 0, first, mid[...])
    per = GRP // 2
    upper = lax.rem(col, 2) == 1
    for t in range(steps):
        x = mul_exact(x, araw[t]) + jnp.where(low, drive[t, :GRP, :], drive[t, GRP:, :])
        xs[t] = x
        filt[t] = jnp.where(upper, x[per:], x[:per])
    proj[...] = mul(xs[...].reshape(steps * GRP, D), dyn[...]).reshape(steps, GRP, D)


def smooth_sweep_kernel(graw, xs, proj, mid, q_m, y_m, s0, s1, s2, s3, smooth):
    tm, core, col = place()
    steps = graw.shape[0]
    got = s0[...] + s1[...] + (s2[...] + s3[...])
    tail = jnp.where(col < 2, y_m[D : D + GRP, :], y_m[D + GRP :, :])
    inner = mul(got, q_m[...]) + (mul(mid[...], y_m[:D, :]) + tail)
    s = jnp.where(core == 0, inner, got)
    per = GRP // 2
    upper = lax.rem(col, 2) == 1
    for t in range(steps - 1, -1, -1):
        s = mul_exact(s - proj[t], graw[t]) + xs[t]
        smooth[t] = jnp.where(upper, s[per:], s[:per])


VM = pl.BlockSpec(memory_space=pltpu.VMEM)


def call(kernel, outs, scratch, *args, grant=8):
    return pl.pallas_call(
        kernel,
        out_shape=tuple(jax.ShapeDtypeStruct(s, d) for s, d in outs),
        in_specs=[VM] * len(args),
        out_specs=tuple(VM for _ in outs),
        scratch_shapes=[pltpu.VMEM(s, d) for s, d in scratch],
        compiler_params=pltpu.CompilerParams(vmem_limit_bytes=grant << 20),
    )(*args)


def local(transition, drive, smoother_gain, dynamics, initial_mean):
    tms, cols = lax.axis_size("tm"), lax.axis_size("col")
    steps = transition.shape[0]
    chips = tms // 2
    square = [((D, D), f32)]
    row_block = ((ROWS, D), f32)

    def send(x, pairs):
        return lax.ppermute(
            x, ("tm", "col"), [(a * cols + b, c * cols + d) for (a, b), (c, d) in pairs]
        )

    def swap(x, lanes=range(4)):
        return send(x, [((i, c), (i ^ 1, c)) for i in range(tms) for c in lanes])

    def turn(x, by):
        return lax.ppermute(x, "col", [(c, (c + by) % 4) for c in range(4)])

    def hop(x, source, target, by=0):
        return send(
            x,
            [
                ((2 * k + h, source), (2 * (k + by) + h, target))
                for k in range(chips)
                for h in range(2)
                if 0 <= k + by < chips
            ],
        )

    def shift(x, dist, lanes):
        pairs = []
        for c in lanes:
            by = dist if c == PRE_X else -dist
            for k in range(chips):
                if 0 <= k + by < chips:
                    pairs += [((2 * k + h, c), (2 * (k + by) + h, c)) for h in range(2)]
        return send(x, pairs)

    extra = jnp.concatenate([drive, initial_mean[None]], 0)
    a_left, g_right = turn(transition, 1), turn(smoother_gain, -1)
    a_right, g_left = turn(transition, -1), turn(smoother_gain, 1)
    a_far, g_far = turn(a_left, 1), turn(g_right, -1)
    e_left, e_right, e_far = turn(extra, 1), turn(extra, -1), turn(extra, 2)

    araw, graw, drive16, xs, x_b, q_b = call(
        forward_kernel,
        [
            ((steps, D, D), bf16),
            ((steps, D, D), bf16),
            ((steps + 1, SER, D), f32),
            ((steps, ALL, D), f32),
            ((ALL, D), f32),
            ((D, D), f32),
        ],
        [],
        transition, a_left, a_right, a_far,
        smoother_gain, g_left, g_right, g_far,
        extra, e_left, e_right, e_far,
        grant=16,
    )
    x_bm, q_bm = swap(x_b), swap(q_b)
    (y_b,) = call(backward_kernel, [((ALL, D), f32)], [], xs, graw, dynamics, grant=16)
    y_bm = swap(y_b)
    own, xrow, qrow, qrow_m = call(
        chip_kernel, [row_block] * 4, [], x_b, x_bm, q_b, q_bm, y_b, y_bm
    )

    dist = 1
    while True:
        last = 2 * dist == chips
        if dist > 1:
            xrow = hop(own, SUF_X, SUF_Y)
            qrow = hop(own, SUF_Q, SUF_Y)
            qrow_m = swap(qrow, (SUF_Y,))
        if last:
            break
        own_m = swap(own, (SUF_Q, PRE_X))
        got = shift(own, dist, range(4))
        got_m = swap(got, (SUF_X, SUF_Y))
        (own,) = call(
            lambda *r, dist=dist: round_kernel(dist, *r),
            [row_block],
            square,
            own, own_m, got, got_m, xrow, qrow, qrow_m,
        )
        dist *= 2

    own_m = swap(own, (SUF_Y, PRE_X))
    got_v = shift(own[HALF:], dist, (PRE_X,))
    got = shift(own, dist, (SUF_Y,))
    (leaving,) = call(mean_kernel, [((GRP, D), f32)], square, own, own_m, got_v)
    x_in = hop(leaving, PRE_X, SUF_Y, 1)
    x_in_m = swap(x_in, (SUF_Y,))
    xrow_m = swap(xrow, (SUF_Y,))
    got_m = swap(got, (SUF_Y,))
    s_lo, s_hi, x_lo, x_hi = call(
        top_kernel,
        [((GRP, D), f32)] * 4,
        square,
        own, own_m, xrow, xrow_m, qrow, qrow_m, got, got_m, x_in, x_in_m,
    )
    s_in = [hop(s_lo if c < 2 else s_hi, SUF_Y, c, -1) for c in range(4)]
    means = [hop(x_lo if c < 2 else x_hi, SUF_Y, c) for c in (0, 2, 3)]
    part = ((steps, GRP, D), f32)
    result = ((steps, drive.shape[1], D), f32)
    xs8, proj, mid, filtered = call(
        mean_sweep_kernel,
        [part, part, ((GRP, D), f32), result],
        [],
        araw, drive16, dynamics, x_b, x_bm, x_lo, *means,
    )
    (smoothed,) = call(
        smooth_sweep_kernel, [result], [], graw, xs8, proj, mid, q_bm, y_bm, *s_in
    )
    return filtered, smoothed


def solution(mesh):
    placed = (P("tm", "col", None), P("tm", "col", None), P("tm", "col", None), P(), P("col", None))
    return jax.shard_map(
        local,
        mesh=mesh,
        in_specs=placed,
        out_specs=(P("tm", "col", None), P("tm", "col", None)),
        check_vma=False,
    )
```

```python
import jax
import jax.numpy as jnp
from jax import lax
from jax.experimental import pallas as pl
from jax.experimental.pallas import tpu as pltpu
from jax.sharding import PartitionSpec as P

SUF_X, SUF_Y, SUF_Q, PRE_X = 0, 1, 2, 3
D = 256
SER = 16
GRP = 8
ALL = D + SER
f32, bf16 = jnp.float32, jnp.bfloat16


def split(x):
    hi = x.astype(bf16)
    return hi, (x - hi.astype(f32)).astype(bf16)


def dot(a, b):
    return jnp.dot(a, b, preferred_element_type=f32)


def mul_exact(x, b):
    hi, lo = split(x)
    return dot(hi, b) + dot(lo, b)


def mul(x, b):
    hi, lo = split(x)
    bhi, blo = split(b)
    return dot(hi, bhi) + (dot(lo, bhi) + dot(hi, blo))


def place():
    tm = lax.axis_index("tm")
    return tm, lax.rem(tm, 2), lax.axis_index("col")


def aligned(index, unit):
    return pl.multiple_of(index * unit, unit)


def assemble(dst, pieces, col):
    rows = pieces[0].shape[1]
    for lag, piece in zip((3, 1, 2), pieces):
        dst[:, pl.ds(aligned(lax.rem(col + lag, 4), rows), rows), :] = piece[...]


def forward_kernel(
    a0, a1, a2, a3, g0, g1, g2, g3, d0, d1, d2, d3, araw, graw, drive, xs, xq_out, sems
):
    tm, core, col = place()
    steps, rows = a1.shape[0], a1.shape[1]
    at = pl.ds(aligned(col, rows), rows)
    copies = [
        pltpu.make_async_copy(a0, araw.at[:, at, :], sems.at[0]),
        pltpu.make_async_copy(g0, graw.at[:, at, :], sems.at[1]),
    ]
    for copy in copies:
        copy.start()
    assemble(araw, (a1, a2, a3), col)
    assemble(graw, (g1, g2, g3), col)
    per = d0.shape[1]
    for c in range(4):

        @pl.when(col == c)
        def _(c=c):
            for lag, piece in zip((0, 3, 1, 2), (d0, d1, d2, d3)):
                first = (c + lag) % 4 * per
                drive[:, first : first + per, :] = piece[...]

    for copy in copies:
        copy.wait()

    @pl.when(tm == lax.axis_size("tm") - 1)
    def _():
        graw[steps - 1] = jnp.zeros((D, D), bf16)

    start = jnp.where(tm == 0, 1.0, 0.0).astype(f32)
    xs[0, :D, :] = araw[0].astype(f32)
    xs[0, D:, :] = mul_exact(drive[steps] * start, araw[0]) + drive[0]
    q = graw[steps - 1].astype(f32)
    for t in range(1, steps):
        new = mul_exact(xs[t - 1], araw[t])
        q = mul_exact(q, graw[steps - 1 - t])
        xs[t, :D, :] = new[:D]
        xs[t, D:, :] = new[D:] + drive[t]
    xq_out[:ALL, :] = xs[steps - 1]
    xq_out[ALL:, :] = q


def backward_kernel(xs, graw, dyn, y_out):
    steps = xs.shape[0]
    dhi, dlo = split(dyn[...])
    s = None
    for t in range(steps - 1, -1, -1):
        x = xs[t]
        hi, lo = split(x)
        proj = dot(hi, dhi) + (dot(lo, dhi) + dot(hi, dlo))
        s = mul_exact(-proj if s is None else s - proj, graw[t]) + x
    y_out[...] = s


def chip_kernel(xq, xq_m, y, y_m, own, xrow, qrow):
    tm, core, col = place()
    x_at, q_at = pl.ds(0, ALL), pl.ds(ALL, D)

    def work(e0, y0, e1, y1):
        x0, q0 = e0[x_at, :], e0[q_at, :]
        new = mul(x0, e1[pl.ds(0, D), :])
        xrow[:D, :] = new[:D]
        xrow[D:, :] = new[D:] + e1[pl.ds(D, SER), :]
        qrow[:D, :] = mul(e1[q_at, :], q0)
        qrow[D:, :] = jnp.zeros((SER, D), f32)
        mid = mul(x0, y1[:D, :])
        mid = jnp.concatenate([mid[:D], mid[D:] + y1[D:, :]], 0)
        new_y = y0[...] + mul(mid, q0)
        own[...] = jnp.where(col == SUF_Y, new_y, jnp.where(col == SUF_Q, qrow[...], xrow[...]))

    @pl.when(core == 0)
    def _():
        work(xq, y, xq_m, y_m)

    @pl.when(core == 1)
    def _():
        work(xq_m, y_m, xq, y)


def round_kernel(dist, own, got, xrow, qrow, out, vec):
    tm, core, col = place()
    chip = lax.div(tm, 2)
    chips = lax.axis_size("tm") // 2

    @pl.when(jnp.logical_or(col == PRE_X, col == SUF_Q))
    def _():
        valid = jnp.where(col == PRE_X, chip >= dist, chip + dist < chips)
        new = mul(got[...], own[:D, :])
        out[:D, :] = jnp.where(valid, new[:D], own[:D, :])
        out[D:, :] = new[D:] + own[D:, :]

    @pl.when(col == SUF_X)
    def _():
        new = mul(own[...], got[:D, :])
        valid = chip + dist < chips
        out[:D, :] = jnp.where(valid, new[:D], own[:D, :])
        out[D:, :] = jnp.where(valid, new[D:] + got[D:, :], own[D:, :])

    @pl.when(col == SUF_Y)
    def _():
        mid = mul(xrow[...], got[:D, :])
        mid = jnp.concatenate([mid[:D], mid[D:] + got[D:, :]], 0)
        out[...] = own[...] + mul(mid, qrow[:D, :])

    vec[...] = out[D:, :]


def mean_kernel(own, got, out):
    out[...] = mul(got[...], own[:D, :]) + own[D:, :]


def top_kernel(own, xrow, qrow, got, begin, s_out):
    x = begin[...]
    s = mul(x, own[:D, :]) + own[D:, :]
    mid = mul(x, xrow[:D, :]) + xrow[D:, :]
    far = mul(mid, got[:D, :]) + got[D:, :]
    s_out[...] = s + mul(far, qrow[:D, :])


def group(value, low):
    return jnp.where(low, value[:GRP], value[GRP:])


def mean_sweep_kernel(araw, drive, dyn, xq_b, xq_bm, x_r, x0, x2, x3, xs, proj, mid, filt):
    tm, core, col = place()
    steps = araw.shape[0]
    low = col < 2
    begin = group(jnp.where(col == SUF_Y, x_r[...], x0[...] + x2[...] + x3[...]), low)

    @pl.when(core == 0)
    def _():
        mid[...] = mul(begin, xq_b[:D, :]) + group(xq_b[D:ALL, :], low)

    @pl.when(core == 1)
    def _():
        mid[...] = mul(begin, xq_bm[:D, :]) + group(xq_bm[D:ALL, :], low)

    first = begin + jnp.where(tm == 0, 1.0, 0.0).astype(f32) * group(drive[steps], low)
    x = jnp.where(core == 0, first, mid[...])
    per = GRP // 2
    upper = lax.rem(col, 2) == 1
    for t in range(steps):
        x = mul_exact(x, araw[t]) + group(drive[t], low)
        xs[t] = x
        filt[t] = jnp.where(upper, x[per:], x[:per])
    proj[...] = mul(xs[...].reshape(steps * GRP, D), dyn[...]).reshape(steps, GRP, D)


def smooth_sweep_kernel(graw, xs, proj, mid, xq_m, y_m, s0, s1, s2, s3, smooth):
    tm, core, col = place()
    steps = graw.shape[0]
    low = col < 2
    got = group(s0[...] + s1[...] + (s2[...] + s3[...]), low)
    inner = mul(got, xq_m[ALL:, :]) + (mul(mid[...], y_m[:D, :]) + group(y_m[D:, :], low))
    s = jnp.where(core == 0, inner, got)
    per = GRP // 2
    upper = lax.rem(col, 2) == 1
    for t in range(steps - 1, -1, -1):
        s = mul_exact(s - proj[t], graw[t]) + xs[t]
        smooth[t] = jnp.where(upper, s[per:], s[:per])


VM = pl.BlockSpec(memory_space=pltpu.VMEM)
ANY = pl.BlockSpec(memory_space=pl.ANY)


def call(kernel, outs, *args, grant=8, scratch=(), plain=()):
    return pl.pallas_call(
        kernel,
        out_shape=tuple(jax.ShapeDtypeStruct(s, d) for s, d in outs),
        in_specs=[ANY if i in plain else VM for i in range(len(args))],
        out_specs=tuple(VM for _ in outs),
        scratch_shapes=list(scratch),
        compiler_params=pltpu.CompilerParams(vmem_limit_bytes=grant << 20),
    )(*args)


def local(transition, drive, smoother_gain, dynamics, initial_mean):
    tms, cols = lax.axis_size("tm"), lax.axis_size("col")
    steps = transition.shape[0]
    chips = tms // 2
    whole, vector = ((ALL, D), f32), ((SER, D), f32)

    def send(x, pairs):
        return lax.ppermute(
            x, ("tm", "col"), [(a * cols + b, c * cols + d) for (a, b), (c, d) in pairs]
        )

    def swap(x):
        return lax.ppermute(x, "tm", [(i, i ^ 1) for i in range(tms)])

    def turn(x, by):
        return lax.ppermute(x, "col", [(c, (c + by) % 4) for c in range(4)])

    def hop(x, source, target, by=0, cores=(0,)):
        return send(
            x,
            [
                ((2 * k + h, source), (2 * (k + by) + h, target))
                for k in range(chips)
                for h in cores
                if 0 <= k + by < chips
            ],
        )

    def shift(x, dist, lanes):
        pairs = []
        for c in lanes:
            by = dist if c == PRE_X else -dist
            for k in range(chips):
                if 0 <= k + by < chips:
                    pairs.append(((2 * k, c), (2 * (k + by), c)))
        return send(x, pairs)

    extra = jnp.concatenate([drive, initial_mean[None]], 0)
    a_left, g_right = turn(transition, 1), turn(smoother_gain, -1)
    a_right, g_left = turn(transition, -1), turn(smoother_gain, 1)
    a_far, g_far = turn(a_left, 1), turn(g_right, -1)
    e_left, e_right, e_far = turn(extra, 1), turn(extra, -1), turn(extra, 2)

    araw, graw, drive16, xs, xq_b = call(
        forward_kernel,
        [
            ((steps, D, D), bf16),
            ((steps, D, D), bf16),
            ((steps + 1, SER, D), f32),
            ((steps, ALL, D), f32),
            ((ALL + D, D), f32),
        ],
        transition, a_left, a_right, a_far,
        smoother_gain, g_left, g_right, g_far,
        extra, e_left, e_right, e_far,
        grant=16,
        plain=(0, 4),
        scratch=[pltpu.SemaphoreType.DMA((2,))],
    )
    xq_bm = swap(xq_b)
    (y_b,) = call(backward_kernel, [whole], xs, graw, dynamics, grant=16)
    y_bm = swap(y_b)
    own, xrow, qrow = call(chip_kernel, [whole] * 3, xq_b, xq_bm, y_b, y_bm)

    dist = 1
    while 2 * dist < chips:
        if dist > 1:
            xrow, qrow = hop(own, SUF_X, SUF_Y), hop(own, SUF_Q, SUF_Y)
        got = shift(own, dist, range(4))
        own, vec = call(
            lambda *r, dist=dist: round_kernel(dist, *r),
            [whole, vector],
            own, got, xrow, qrow,
        )
        dist *= 2

    got_v = shift(vec, dist, (PRE_X,))
    (leaving,) = call(mean_kernel, [vector], own, got_v)
    x_in = hop(leaving, PRE_X, SUF_Y, 1)
    got = shift(own, dist, (SUF_Y,))
    xrow, qrow = hop(own, SUF_X, SUF_Y), hop(own, SUF_Q, SUF_Y)
    (s_out,) = call(top_kernel, [vector], own, xrow, qrow, got, x_in)

    def on_both(x):
        return jnp.where(lax.rem(lax.axis_index("tm"), 2) == 0, x, swap(x))

    x_both, s_both = on_both(x_in), on_both(s_out)
    s_in = [hop(s_both, SUF_Y, c, -1, (0, 1)) for c in range(4)]
    means = [hop(x_both, SUF_Y, c, 0, (0, 1)) for c in (0, 2, 3)]
    part = ((steps, GRP, D), f32)
    result = ((steps, drive.shape[1], D), f32)
    xs8, proj, mid, filtered = call(
        mean_sweep_kernel,
        [part, part, ((GRP, D), f32), result],
        araw, drive16, dynamics, xq_b, xq_bm, x_both, *means,
    )
    (smoothed,) = call(
        smooth_sweep_kernel, [result], graw, xs8, proj, mid, xq_bm, y_bm, *s_in
    )
    return filtered, smoothed


def solution(mesh):
    placed = (P("tm", "col", None), P("tm", "col", None), P("tm", "col", None), P(), P("col", None))
    return jax.shard_map(
        local,
        mesh=mesh,
        in_specs=placed,
        out_specs=(P("tm", "col", None), P("tm", "col", None)),
        check_vma=False,
    )
```

```python
import jax
import jax.numpy as jnp
from jax import lax
from jax.experimental import pallas as pl
from jax.experimental.pallas import tpu as pltpu
from jax.sharding import PartitionSpec as P


SUF_X, SUF_Y, SUF_Q = (0, 0), (1, 0), (2, 0)
PRE_X = (1, 1)
D = 256
SER = 16
GRP = 8
ALL = D + SER
f32, bf16 = jnp.float32, jnp.bfloat16


def split(x):
    hi = x.astype(bf16)
    return hi, (x - hi.astype(f32)).astype(bf16)


def dot(a, b):
    return jnp.dot(a, b, preferred_element_type=f32)


def mul_exact(x, b):
    hi, lo = split(x)
    return dot(hi, b) + dot(lo, b)


def mul(x, b):
    hi, lo = split(x)
    bhi, blo = split(b)
    return dot(hi, bhi) + (dot(lo, bhi) + dot(hi, blo))


def place():
    tm = lax.axis_index("tm")
    return tm, lax.rem(tm, 2), lax.axis_index("col")


def roles(core, col):
    return col == 0, jnp.logical_and(col == 1, core == 0), jnp.logical_and(col == 1, core == 1)


def aligned(index, unit):
    return pl.multiple_of(index * unit, unit)


def assemble(dst, pieces, col):
    rows = pieces[0].shape[1]
    for lag, piece in zip((0, 3, 1, 2), pieces):
        dst[:, pl.ds(aligned(lax.rem(col + lag, 4), rows), rows), :] = piece[...]


def stage_kernel(a, g, dyn, a_out, g_out, dyn_out):
    a_out[...] = a[...]
    g_out[...] = g[...]
    dyn_out[...] = dyn[...]


def forward_kernel(a0, a1, a2, a3, d0, d1, d2, d3, dyn, araw, drive, xs, proj, x_out):
    tm, _, col = place()
    steps = a0.shape[0]
    assemble(araw, (a0, a1, a2, a3), col)
    per = d0.shape[1]
    for c in range(4):

        @pl.when(col == c)
        def _(c=c):
            for lag, piece in zip((0, 3, 1, 2), (d0, d1, d2, d3)):
                first = (c + lag) % 4 * per
                drive[:, first : first + per, :] = piece[...]

    start = jnp.where(tm == 0, 1.0, 0.0).astype(f32)
    dhi, dlo = split(dyn[...])
    for t in range(steps):
        if t == 0:
            xs[0, :D, :] = araw[0].astype(f32)
            xs[0, D:, :] = mul_exact(drive[steps] * start, araw[0]) + drive[0]
        else:
            new = mul_exact(xs[t - 1], araw[t])
            xs[t, :D, :] = new[:D]
            xs[t, D:, :] = new[D:] + drive[t]
        hi, lo = split(xs[t])
        proj[t] = dot(hi, dhi) + (dot(lo, dhi) + dot(hi, dlo))
    x_out[...] = xs[steps - 1]


def backward_kernel(g0, g1, g2, g3, xs, proj, graw, qy_out):
    tm, _, col = place()
    steps = g0.shape[0]
    assemble(graw, (g0, g1, g2, g3), col)

    @pl.when(tm == lax.axis_size("tm") - 1)
    def _():
        graw[steps - 1] = jnp.zeros((D, D), bf16)

    g = graw[steps - 1]
    q = g.astype(f32)
    s = mul_exact(-proj[steps - 1], g) + xs[steps - 1]
    for t in range(steps - 2, -1, -1):
        g = graw[t]
        q = mul_exact(q, g)
        s = mul_exact(s - proj[t], g) + xs[t]
    qy_out[:D, :] = q
    qy_out[D:, :] = s


def chip_kernel(x, x_m, qy, qy_m, own, xrow, qrow):
    _, core, col = place()
    suf_x, suf_y, pre_x = roles(core, col)

    def work(x0_ref, e0, x1, e1):
        x0, q0 = x0_ref[...], e0[:D, :]
        new = mul(x0, x1[:D, :])
        xrow[:D, :] = new[:D]
        xrow[D:, :] = new[D:] + x1[D:, :]
        qrow[:D, :] = mul(e1[:D, :], q0)
        qrow[D:, :] = jnp.zeros((SER, D), f32)
        mid = mul(x0, e1[D : 2 * D, :])
        mid = jnp.concatenate([mid[:D], mid[D:] + e1[2 * D :, :]], 0)
        new_y = e0[D:, :] + mul(mid, q0)
        rest = jnp.where(jnp.logical_or(suf_x, pre_x), xrow[...], qrow[...])
        own[...] = jnp.where(suf_y, new_y, rest)

    @pl.when(core == 0)
    def _():
        work(x, qy, x_m, qy_m)

    @pl.when(core == 1)
    def _():
        work(x_m, qy_m, x, qy)


def round_kernel(dist, own, got, xrow, qrow, kept_a, kept_d, out, vec):
    tm, core, col = place()
    suf_x, suf_y, pre_x = roles(core, col)
    chip = lax.div(tm, 2)
    later = chip + dist < lax.axis_size("tm") // 2

    @pl.when(jnp.logical_not(jnp.logical_or(suf_x, suf_y)))
    def _():
        valid = jnp.where(pre_x, chip >= dist, later)
        new = mul(got[...], own[:D, :])
        out[:D, :] = jnp.where(valid, new[:D], own[:D, :])
        out[D:, :] = new[D:] + own[D:, :]

    @pl.when(suf_x)
    def _():
        new = mul(own[...], got[:D, :])
        out[:D, :] = jnp.where(later, new[:D], own[:D, :])
        out[D:, :] = jnp.where(later, new[D:] + got[D:, :], own[D:, :])

    @pl.when(suf_y)
    def _():
        mid = mul(xrow[...], got[:D, :])
        mid = jnp.concatenate([mid[:D], mid[D:] + got[D:, :]], 0)
        out[...] = own[...] + mul(mid, qrow[:D, :])

    vec[...] = out[D:, :]


def mean_kernel(own, got, out):
    out[...] = mul(got[...], own[:D, :]) + own[D:, :]


def near_kernel(own, xrow, begin, near, mid):
    x = begin[...]
    near[...] = mul(x, own[:D, :]) + own[D:, :]
    mid[...] = mul(x, xrow[:D, :]) + xrow[D:, :]


def top_kernel(near, mid, qrow, got, s_out):
    far = mul(mid[...], got[:D, :]) + got[D:, :]
    s_out[...] = near[...] + mul(far, qrow[:D, :])


def group(value, low):
    return jnp.where(low, value[:GRP], value[GRP:])


def mean_sweep_kernel(araw, drive, dyn, x_b, x_bm, x_r, x0, x2, x3, xs, proj, mid, filt):
    tm, core, col = place()
    steps = araw.shape[0]
    low = col < 2
    begin = group(jnp.where(col == 1, x_r[...], x0[...] + x2[...] + x3[...]), low)

    @pl.when(core == 0)
    def _():
        mid[...] = mul(begin, x_b[:D, :]) + group(x_b[D:, :], low)

    @pl.when(core == 1)
    def _():
        mid[...] = mul(begin, x_bm[:D, :]) + group(x_bm[D:, :], low)

    first = begin + jnp.where(tm == 0, 1.0, 0.0).astype(f32) * group(drive[steps], low)
    x = jnp.where(core == 0, first, mid[...])
    per = GRP // 2
    upper = lax.rem(col, 2) == 1
    for t in range(steps):
        x = mul_exact(x, araw[t]) + group(drive[t], low)
        xs[t] = x
        filt[t] = jnp.where(upper, x[per:], x[:per])
    proj[...] = mul(xs[...].reshape(steps * GRP, D), dyn[...]).reshape(steps, GRP, D)


def smooth_sweep_kernel(graw, xs, proj, mid, qy_m, s0, s1, s2, s3, smooth):
    _, core, col = place()
    steps = graw.shape[0]
    low = col < 2
    got = group(s0[...] + s1[...] + (s2[...] + s3[...]), low)
    inner = mul(got, qy_m[:D, :]) + (
        mul(mid[...], qy_m[D : 2 * D, :]) + group(qy_m[2 * D :, :], low)
    )
    s = jnp.where(core == 0, inner, got)
    per = GRP // 2
    upper = lax.rem(col, 2) == 1
    for t in range(steps - 1, -1, -1):
        s = mul_exact(s - proj[t], graw[t]) + xs[t]
        smooth[t] = jnp.where(upper, s[per:], s[:per])


VM = pl.BlockSpec(memory_space=pltpu.VMEM)


def call(kernel, outs, *args, grant=8):
    return pl.pallas_call(
        kernel,
        out_shape=tuple(jax.ShapeDtypeStruct(s, d) for s, d in outs),
        in_specs=[VM] * len(args),
        out_specs=tuple(VM for _ in outs),
        compiler_params=pltpu.CompilerParams(vmem_limit_bytes=grant << 20),
    )(*args)


def scan(transition, drive, smoother_gain, dynamics, initial_mean):
    tms, cols = lax.axis_size("tm"), lax.axis_size("col")
    steps = transition.shape[0]
    chips = tms // 2
    whole, vector = ((ALL, D), f32), ((SER, D), f32)

    def send(x, pairs):
        return lax.ppermute(
            x, ("tm", "col"), [(a * cols + b, c * cols + d) for (a, b), (c, d) in pairs]
        )

    def swap(x):
        return lax.ppermute(x, "tm", [(i, i ^ 1) for i in range(tms)])

    def turn(x, by):
        return lax.ppermute(x, "col", [(c, (c + by) % 4) for c in range(4)])

    def hop(x, moves, by=0):
        return send(
            x,
            [
                ((2 * k + h, c), (2 * (k + by) + g, d))
                for k in range(chips)
                for (c, h), (d, g) in moves
                if 0 <= k + by < chips
            ],
        )

    def shift(x, dist, lanes):
        pairs = []
        for c, h in lanes:
            by = dist if (c, h) == PRE_X else -dist
            for k in range(chips):
                if 0 <= k + by < chips:
                    pairs.append(((2 * k + h, c), (2 * (k + by) + h, c)))
        return send(x, pairs)

    def across(c):
        return [((1, h), (c, h)) for h in range(2)]

    extra = jnp.concatenate([drive, initial_mean[None]], 0)
    a_left, a_right = turn(transition, 1), turn(transition, -1)
    a_far = turn(a_left, 1)
    g_right, g_left = turn(smoother_gain, -1), turn(smoother_gain, 1)
    g_far = turn(g_right, -1)
    e_left, e_right, e_far = turn(extra, 1), turn(extra, -1), turn(extra, 2)

    quarter = (transition.shape, bf16)
    a_own, g_own, dyn = call(
        stage_kernel, [quarter, quarter, ((D, D), f32)], transition, smoother_gain, dynamics
    )
    araw, drive16, xs, proj, x_b = call(
        forward_kernel,
        [
            ((steps, D, D), bf16),
            ((steps + 1, SER, D), f32),
            ((steps, ALL, D), f32),
            ((steps, ALL, D), f32),
            whole,
        ],
        a_own, a_left, a_right, a_far,
        extra, e_left, e_right, e_far, dyn,
        grant=16,
    )
    x_bm = swap(x_b)
    graw, qy_b = call(
        backward_kernel,
        [((steps, D, D), bf16), ((ALL + D, D), f32)],
        g_own, g_left, g_right, g_far, xs, proj,
        grant=16,
    )
    qy_bm = swap(qy_b)
    own, xrow, qrow = call(chip_kernel, [whole] * 3, x_b, x_bm, qy_b, qy_bm)

    dist = 1
    while 2 * dist < chips:
        if dist > 1:
            xrow = hop(own, [(SUF_X, SUF_Y)])
            qrow = hop(own, [(SUF_Q, SUF_Y)])
        got = shift(own, dist, (SUF_X, SUF_Y, SUF_Q, PRE_X))
        own, vec = call(
            lambda *r, dist=dist: round_kernel(dist, *r),
            [whole, vector],
            own, got, xrow, qrow, araw, drive16,
        )
        dist *= 2

    got_v = shift(vec, dist, (PRE_X,))
    got = shift(own, dist, (SUF_Y,))
    xrow = hop(own, [(SUF_X, SUF_Y)])
    qrow = hop(own, [(SUF_Q, SUF_Y)])
    (leaving,) = call(mean_kernel, [vector], own, got_v)
    x_one = hop(leaving, [(PRE_X, PRE_X)], 1)
    first = lax.rem(lax.axis_index("tm"), 2) == 0
    x_two = jnp.where(first, hop(x_one, [(PRE_X, SUF_Y)]), x_one)
    means = [hop(x_two, across(c)) for c in (3, 0, 2)]
    near, mid = call(near_kernel, [vector, vector], own, xrow, x_two)
    (s_one,) = call(top_kernel, [vector], near, mid, qrow, got)
    s_two = jnp.where(first, s_one, hop(s_one, [(SUF_Y, PRE_X)]))
    s_in = [hop(s_two, across(c), -1) for c in (3, 0, 2, 1)]
    part = ((steps, GRP, D), f32)
    result = ((steps, drive.shape[1], D), f32)
    xs8, proj8, mid8, filtered = call(
        mean_sweep_kernel,
        [part, part, ((GRP, D), f32), result],
        araw, drive16, dyn, x_b, x_bm, x_two, *means,
    )
    (smoothed,) = call(smooth_sweep_kernel, [result], graw, xs8, proj8, mid8, qy_bm, *s_in)
    return filtered, smoothed


def solution(mesh):
    placed = (P("tm", "col", None), P("tm", "col", None), P("tm", "col", None), P(), P("col", None))
    return jax.shard_map(
        scan,
        mesh=mesh,
        in_specs=placed,
        out_specs=(P("tm", "col", None), P("tm", "col", None)),
        check_vma=False,
    )
```

```python
import jax
import jax.numpy as jnp
from jax import lax
from jax.experimental import pallas as pl
from jax.experimental.pallas import tpu as pltpu
from jax.sharding import PartitionSpec as P


SUF_X, SUF_Y, SUF_Q = (0, 0), (1, 0), (2, 0)
PRE_X = (3, 0)
D = 256
SER = 16
GRP = 8
ALL = D + SER
f32, bf16 = jnp.float32, jnp.bfloat16


def split(x):
    hi = x.astype(bf16)
    return hi, (x - hi.astype(f32)).astype(bf16)


def dot(a, b):
    return jnp.dot(a, b, preferred_element_type=f32)


def mul_exact(x, b):
    hi, lo = split(x)
    return dot(hi, b) + dot(lo, b)


def mul(x, b):
    hi, lo = split(x)
    bhi, blo = split(b)
    return dot(hi, bhi) + (dot(lo, bhi) + dot(hi, blo))


def place():
    tm = lax.axis_index("tm")
    return tm, lax.rem(tm, 2), lax.axis_index("col")


def roles(col):
    return col == 0, col == 1, col == 3


def aligned(index, unit):
    return pl.multiple_of(index * unit, unit)


def assemble(dst, pieces, col):
    rows = pieces[0].shape[1]
    for lag, piece in zip((0, 3, 1, 2), pieces):
        dst[:, pl.ds(aligned(lax.rem(col + lag, 4), rows), rows), :] = piece[...]


def stage_kernel(a, g, dyn, a_out, g_out, dyn_out):
    a_out[...] = a[...]
    g_out[...] = g[...]
    dyn_out[...] = dyn[...]


def forward_kernel(a0, a1, a2, a3, d0, d1, d2, d3, dyn, araw, drive, xs, proj, x_out):
    tm, _, col = place()
    steps = a0.shape[0]
    assemble(araw, (a0, a1, a2, a3), col)
    per = d0.shape[1]
    for c in range(4):

        @pl.when(col == c)
        def _(c=c):
            for lag, piece in zip((0, 3, 1, 2), (d0, d1, d2, d3)):
                first = (c + lag) % 4 * per
                drive[:, first : first + per, :] = piece[...]

    start = jnp.where(tm == 0, 1.0, 0.0).astype(f32)
    dhi, dlo = split(dyn[...])
    for t in range(steps):
        if t == 0:
            xs[0, :D, :] = araw[0].astype(f32)
            xs[0, D:, :] = mul_exact(drive[steps] * start, araw[0]) + drive[0]
        else:
            new = mul_exact(xs[t - 1], araw[t])
            xs[t, :D, :] = new[:D]
            xs[t, D:, :] = new[D:] + drive[t]
        hi, lo = split(xs[t])
        proj[t] = dot(hi, dhi) + (dot(lo, dhi) + dot(hi, dlo))
    x_out[...] = xs[steps - 1]


def backward_kernel(g0, g1, g2, g3, xs, proj, graw, qy_out):
    tm, _, col = place()
    steps = g0.shape[0]
    assemble(graw, (g0, g1, g2, g3), col)

    @pl.when(tm == lax.axis_size("tm") - 1)
    def _():
        graw[steps - 1] = jnp.zeros((D, D), bf16)

    g = graw[steps - 1]
    q = g.astype(f32)
    s = mul_exact(-proj[steps - 1], g) + xs[steps - 1]
    for t in range(steps - 2, -1, -1):
        g = graw[t]
        q = mul_exact(q, g)
        s = mul_exact(s - proj[t], g) + xs[t]
    qy_out[:D, :] = q
    qy_out[D:, :] = s


def chip_kernel(x, x_m, qy, qy_m, own, xrow, qrow):
    _, core, col = place()
    suf_x, suf_y, pre_x = roles(col)

    def work(x0_ref, e0, x1, e1):
        x0, q0 = x0_ref[...], e0[:D, :]
        new = mul(x0, x1[:D, :])
        xrow[:D, :] = new[:D]
        xrow[D:, :] = new[D:] + x1[D:, :]
        qrow[:D, :] = mul(e1[:D, :], q0)
        qrow[D:, :] = jnp.zeros((SER, D), f32)
        mid = mul(x0, e1[D : 2 * D, :])
        mid = jnp.concatenate([mid[:D], mid[D:] + e1[2 * D :, :]], 0)
        new_y = e0[D:, :] + mul(mid, q0)
        rest = jnp.where(jnp.logical_or(suf_x, pre_x), xrow[...], qrow[...])
        own[...] = jnp.where(suf_y, new_y, rest)

    @pl.when(core == 0)
    def _():
        work(x, qy, x_m, qy_m)

    @pl.when(core == 1)
    def _():
        work(x_m, qy_m, x, qy)


def round_kernel(dist, own, got, xrow, qrow, kept_a, kept_d, out, vec):
    tm, _, col = place()
    suf_x, suf_y, pre_x = roles(col)
    chip = lax.div(tm, 2)
    later = chip + dist < lax.axis_size("tm") // 2

    @pl.when(jnp.logical_not(jnp.logical_or(suf_x, suf_y)))
    def _():
        valid = jnp.where(pre_x, chip >= dist, later)
        new = mul(got[...], own[:D, :])
        out[:D, :] = jnp.where(valid, new[:D], own[:D, :])
        out[D:, :] = new[D:] + own[D:, :]

    @pl.when(suf_x)
    def _():
        new = mul(own[...], got[:D, :])
        out[:D, :] = jnp.where(later, new[:D], own[:D, :])
        out[D:, :] = jnp.where(later, new[D:] + got[D:, :], own[D:, :])

    @pl.when(suf_y)
    def _():
        mid = mul(xrow[...], got[:D, :])
        mid = jnp.concatenate([mid[:D], mid[D:] + got[D:, :]], 0)
        out[...] = own[...] + mul(mid, qrow[:D, :])

    vec[...] = out[D:, :]


def mean_kernel(own, got, out):
    out[...] = mul(got[...], own[:D, :]) + own[D:, :]


def near_kernel(own, xrow, begin, near, mid):
    x = begin[...]
    near[...] = mul(x, own[:D, :]) + own[D:, :]
    mid[...] = mul(x, xrow[:D, :]) + xrow[D:, :]


def top_kernel(near, mid, qrow, got, s_out):
    far = mul(mid[...], got[:D, :]) + got[D:, :]
    s_out[...] = near[...] + mul(far, qrow[:D, :])


def group(value, low):
    return jnp.where(low, value[:GRP], value[GRP:])


def mean_sweep_kernel(araw, drive, dyn, x_b, x_bm, m0, m1, m2, m3, m4, xs, proj, mid, filt):
    tm, core, col = place()
    steps = araw.shape[0]
    low = col < 2
    begin = group((m0[...] + m1[...]) + (m2[...] + m3[...]) + m4[...], low)

    @pl.when(core == 0)
    def _():
        mid[...] = mul(begin, x_b[:D, :]) + group(x_b[D:, :], low)

    @pl.when(core == 1)
    def _():
        mid[...] = mul(begin, x_bm[:D, :]) + group(x_bm[D:, :], low)

    first = begin + jnp.where(tm == 0, 1.0, 0.0).astype(f32) * group(drive[steps], low)
    x = jnp.where(core == 0, first, mid[...])
    per = GRP // 2
    upper = lax.rem(col, 2) == 1
    for t in range(steps):
        x = mul_exact(x, araw[t]) + group(drive[t], low)
        xs[t] = x
        filt[t] = jnp.where(upper, x[per:], x[:per])
    proj[...] = mul(xs[...].reshape(steps * GRP, D), dyn[...]).reshape(steps, GRP, D)


def smooth_sweep_kernel(graw, xs, proj, mid, qy_m, s0, s1, s2, s3, smooth):
    _, core, col = place()
    steps = graw.shape[0]
    low = col < 2
    got = group(s0[...] + s1[...] + (s2[...] + s3[...]), low)
    inner = mul(got, qy_m[:D, :]) + (
        mul(mid[...], qy_m[D : 2 * D, :]) + group(qy_m[2 * D :, :], low)
    )
    s = jnp.where(core == 0, inner, got)
    per = GRP // 2
    upper = lax.rem(col, 2) == 1
    for t in range(steps - 1, -1, -1):
        s = mul_exact(s - proj[t], graw[t]) + xs[t]
        smooth[t] = jnp.where(upper, s[per:], s[:per])


VM = pl.BlockSpec(memory_space=pltpu.VMEM)


def call(kernel, outs, *args, grant=8):
    return pl.pallas_call(
        kernel,
        out_shape=tuple(jax.ShapeDtypeStruct(s, d) for s, d in outs),
        in_specs=[VM] * len(args),
        out_specs=tuple(VM for _ in outs),
        compiler_params=pltpu.CompilerParams(vmem_limit_bytes=grant << 20),
    )(*args)


def scan(transition, drive, smoother_gain, dynamics, initial_mean):
    tms, cols = lax.axis_size("tm"), lax.axis_size("col")
    steps = transition.shape[0]
    chips = tms // 2
    whole, vector = ((ALL, D), f32), ((SER, D), f32)

    def send(x, pairs):
        return lax.ppermute(
            x, ("tm", "col"), [(a * cols + b, c * cols + d) for (a, b), (c, d) in pairs]
        )

    def swap(x):
        return lax.ppermute(x, "tm", [(i, i ^ 1) for i in range(tms)])

    def turn(x, by):
        return lax.ppermute(x, "col", [(c, (c + by) % 4) for c in range(4)])

    def hop(x, moves, by=0):
        return send(
            x,
            [
                ((2 * k + h, c), (2 * (k + by) + g, d))
                for k in range(chips)
                for (c, h), (d, g) in moves
                if 0 <= k + by < chips
            ],
        )

    def shift(x, dist, lanes):
        pairs = []
        for c, h in lanes:
            by = dist if (c, h) == PRE_X else -dist
            for k in range(chips):
                if 0 <= k + by < chips:
                    pairs.append(((2 * k + h, c), (2 * (k + by) + h, c)))
        return send(x, pairs)

    def across(c):
        return [((1, h), (c, h)) for h in range(2)]

    extra = jnp.concatenate([drive, initial_mean[None]], 0)
    a_left, a_right = turn(transition, 1), turn(transition, -1)
    a_far = turn(a_left, 1)
    g_right, g_left = turn(smoother_gain, -1), turn(smoother_gain, 1)
    g_far = turn(g_right, -1)
    e_left, e_right, e_far = turn(extra, 1), turn(extra, -1), turn(extra, 2)

    quarter = (transition.shape, bf16)
    a_own, g_own, dyn = call(
        stage_kernel, [quarter, quarter, ((D, D), f32)], transition, smoother_gain, dynamics
    )
    araw, drive16, xs, proj, x_b = call(
        forward_kernel,
        [
            ((steps, D, D), bf16),
            ((steps + 1, SER, D), f32),
            ((steps, ALL, D), f32),
            ((steps, ALL, D), f32),
            whole,
        ],
        a_own, a_left, a_right, a_far,
        extra, e_left, e_right, e_far, dyn,
        grant=16,
    )
    x_bm = swap(x_b)
    graw, qy_b = call(
        backward_kernel,
        [((steps, D, D), bf16), ((ALL + D, D), f32)],
        g_own, g_left, g_right, g_far, xs, proj,
        grant=16,
    )
    qy_bm = swap(qy_b)
    own, xrow, qrow = call(chip_kernel, [whole] * 3, x_b, x_bm, qy_b, qy_bm)

    dist = 1
    while 2 * dist < chips:
        if dist > 1:
            xrow = hop(own, [(SUF_X, SUF_Y)])
            qrow = hop(own, [(SUF_Q, SUF_Y)])
        got = shift(own, dist, (SUF_X, SUF_Y, SUF_Q, PRE_X))
        own, vec = call(
            lambda *r, dist=dist: round_kernel(dist, *r),
            [whole, vector],
            own, got, xrow, qrow, araw, drive16,
        )
        dist *= 2

    got_v = shift(vec, dist, (PRE_X,))
    got = shift(own, dist, (SUF_Y,))
    xrow = hop(own, [(SUF_X, SUF_Y)])
    qrow = hop(own, [(SUF_Q, SUF_Y)])
    (leaving,) = call(mean_kernel, [vector], own, got_v)
    means = [hop(leaving, [(PRE_X, (c, 0))], 1) for c in range(4)]
    begin = means[1]
    means.append(hop(sum(means), [((c, 0), (c, 1)) for c in range(4)]))
    first = lax.rem(lax.axis_index("tm"), 2) == 0
    near, mid = call(near_kernel, [vector, vector], own, xrow, begin)
    (s_one,) = call(top_kernel, [vector], near, mid, qrow, got)
    s_two = jnp.where(first, s_one, hop(s_one, [(SUF_Y, (1, 1))]))
    s_in = [hop(s_two, across(c), -1) for c in (3, 0, 2, 1)]
    part = ((steps, GRP, D), f32)
    result = ((steps, drive.shape[1], D), f32)
    xs8, proj8, mid8, filtered = call(
        mean_sweep_kernel,
        [part, part, ((GRP, D), f32), result],
        araw, drive16, dyn, x_b, x_bm, *means,
    )
    (smoothed,) = call(smooth_sweep_kernel, [result], graw, xs8, proj8, mid8, qy_bm, *s_in)
    return filtered, smoothed


def solution(mesh):
    placed = (P("tm", "col", None), P("tm", "col", None), P("tm", "col", None), P(), P("col", None))
    return jax.shard_map(
        scan,
        mesh=mesh,
        in_specs=placed,
        out_specs=(P("tm", "col", None), P("tm", "col", None)),
        check_vma=False,
    )
```

```python
import jax
import jax.numpy as jnp
from jax import lax
from jax.experimental import pallas as pl
from jax.experimental.pallas import tpu as pltpu
from jax.sharding import PartitionSpec as P


SUF_X, SUF_Y, SUF_Q = (0, 0), (1, 0), (2, 0)
PRE_X = (3, 0)
D = 256
SER = 16
GRP = 8
ALL = D + SER
f32, bf16 = jnp.float32, jnp.bfloat16


def split(x):
    hi = x.astype(bf16)
    return hi, (x - hi.astype(f32)).astype(bf16)


def dot(a, b):
    return jnp.dot(a, b, preferred_element_type=f32)


def mul_exact(x, b):
    hi, lo = split(x)
    return dot(hi, b) + dot(lo, b)


def mul(x, b):
    hi, lo = split(x)
    bhi, blo = split(b)
    return dot(hi, bhi) + (dot(lo, bhi) + dot(hi, blo))


def place():
    tm = lax.axis_index("tm")
    return tm, lax.rem(tm, 2), lax.axis_index("col")


def roles(col):
    return col == 0, col == 1, col == 3


def aligned(index, unit):
    return pl.multiple_of(index * unit, unit)


def assemble(dst, pieces, col):
    rows = pieces[0].shape[1]
    for lag, piece in zip((0, 3, 1, 2), pieces):
        dst[:, pl.ds(aligned(lax.rem(col + lag, 4), rows), rows), :] = piece[...]


def stage_kernel(a, g, dyn, a_out, g_out, dyn_out):
    a_out[...] = a[...]
    g_out[...] = g[...]
    dyn_out[...] = dyn[...]


def forward_kernel(a0, a1, a2, a3, d0, d1, d2, d3, dyn, araw, drive, xs, proj, x_out):
    tm, _, col = place()
    steps = a0.shape[0]
    assemble(araw, (a0, a1, a2, a3), col)
    per = d0.shape[1]
    for c in range(4):

        @pl.when(col == c)
        def _(c=c):
            for lag, piece in zip((0, 3, 1, 2), (d0, d1, d2, d3)):
                first = (c + lag) % 4 * per
                drive[:, first : first + per, :] = piece[...]

    start = jnp.where(tm == 0, 1.0, 0.0).astype(f32)
    dhi, dlo = split(dyn[...])
    for t in range(steps):
        if t == 0:
            xs[0, :D, :] = araw[0].astype(f32)
            xs[0, D:, :] = mul_exact(drive[steps] * start, araw[0]) + drive[0]
        else:
            new = mul_exact(xs[t - 1], araw[t])
            xs[t, :D, :] = new[:D]
            xs[t, D:, :] = new[D:] + drive[t]
        hi, lo = split(xs[t])
        proj[t] = dot(hi, dhi) + (dot(lo, dhi) + dot(hi, dlo))
    x_out[...] = xs[steps - 1]


def backward_kernel(g0, g1, g2, g3, xs, proj, graw, qy_out):
    tm, _, col = place()
    steps = g0.shape[0]
    assemble(graw, (g0, g1, g2, g3), col)

    @pl.when(tm == lax.axis_size("tm") - 1)
    def _():
        graw[steps - 1] = jnp.zeros((D, D), bf16)

    g = graw[steps - 1]
    q = g.astype(f32)
    s = mul_exact(-proj[steps - 1], g) + xs[steps - 1]
    for t in range(steps - 2, -1, -1):
        g = graw[t]
        q = mul_exact(q, g)
        s = mul_exact(s - proj[t], g) + xs[t]
    qy_out[:D, :] = q
    qy_out[D:, :] = s


def chip_kernel(x, x_m, qy, qy_m, own, xrow, qrow):
    _, core, col = place()
    suf_x, suf_y, pre_x = roles(col)

    def work(x0_ref, e0, x1, e1):
        x0, q0 = x0_ref[...], e0[:D, :]
        new = mul(x0, x1[:D, :])
        xrow[:D, :] = new[:D]
        xrow[D:, :] = new[D:] + x1[D:, :]
        qrow[:D, :] = mul(e1[:D, :], q0)
        qrow[D:, :] = jnp.zeros((SER, D), f32)
        mid = mul(x0, e1[D : 2 * D, :])
        mid = jnp.concatenate([mid[:D], mid[D:] + e1[2 * D :, :]], 0)
        new_y = e0[D:, :] + mul(mid, q0)
        rest = jnp.where(jnp.logical_or(suf_x, pre_x), xrow[...], qrow[...])
        own[...] = jnp.where(suf_y, new_y, rest)

    @pl.when(core == 0)
    def _():
        work(x, qy, x_m, qy_m)

    @pl.when(core == 1)
    def _():
        work(x_m, qy_m, x, qy)


def round_kernel(dist, own, got, xrow, qrow, kept_a, kept_d, kept_g, out, vec):
    tm, _, col = place()
    suf_x, suf_y, pre_x = roles(col)
    chip = lax.div(tm, 2)
    later = chip + dist < lax.axis_size("tm") // 2

    @pl.when(jnp.logical_not(jnp.logical_or(suf_x, suf_y)))
    def _():
        valid = jnp.where(pre_x, chip >= dist, later)
        new = mul(got[...], own[:D, :])
        out[:D, :] = jnp.where(valid, new[:D], own[:D, :])
        out[D:, :] = new[D:] + own[D:, :]

    @pl.when(suf_x)
    def _():
        new = mul(own[...], got[:D, :])
        out[:D, :] = jnp.where(later, new[:D], own[:D, :])
        out[D:, :] = jnp.where(later, new[D:] + got[D:, :], own[D:, :])

    @pl.when(suf_y)
    def _():
        mid = mul(xrow[...], got[:D, :])
        mid = jnp.concatenate([mid[:D], mid[D:] + got[D:, :]], 0)
        out[...] = own[...] + mul(mid, qrow[:D, :])

    vec[...] = out[D:, :]


def mean_kernel(own, got, out):
    out[...] = mul(got[...], own[:D, :]) + own[D:, :]


def near_kernel(own, xrow, begin, near, mid):
    x = begin[...]
    near[...] = mul(x, own[:D, :]) + own[D:, :]
    mid[...] = mul(x, xrow[:D, :]) + xrow[D:, :]


def top_kernel(near, mid, qrow, got, s_out):
    far = mul(mid[...], got[:D, :]) + got[D:, :]
    s_out[...] = near[...] + mul(far, qrow[:D, :])


def group(value, low):
    return jnp.where(low, value[:GRP], value[GRP:])


def mean_sweep_kernel(araw, drive, dyn, x_b, x_bm, m0, m1, m2, m3, m4, xs, proj, mid, filt):
    tm, core, col = place()
    steps = araw.shape[0]
    low = col < 2
    begin = group((m0[...] + m1[...]) + (m2[...] + m3[...]) + m4[...], low)

    @pl.when(core == 0)
    def _():
        mid[...] = mul(begin, x_b[:D, :]) + group(x_b[D:, :], low)

    @pl.when(core == 1)
    def _():
        mid[...] = mul(begin, x_bm[:D, :]) + group(x_bm[D:, :], low)

    first = begin + jnp.where(tm == 0, 1.0, 0.0).astype(f32) * group(drive[steps], low)
    x = jnp.where(core == 0, first, mid[...])
    per = GRP // 2
    upper = lax.rem(col, 2) == 1
    for t in range(steps):
        x = mul_exact(x, araw[t]) + group(drive[t], low)
        xs[t] = x
        filt[t] = jnp.where(upper, x[per:], x[:per])
    proj[...] = mul(xs[...].reshape(steps * GRP, D), dyn[...]).reshape(steps, GRP, D)


def smooth_sweep_kernel(graw, xs, proj, mid, qy_m, s0, s1, s2, s3, smooth):
    _, core, col = place()
    steps = graw.shape[0]
    low = col < 2
    got = group(s0[...] + s1[...] + (s2[...] + s3[...]), low)
    inner = mul(got, qy_m[:D, :]) + (
        mul(mid[...], qy_m[D : 2 * D, :]) + group(qy_m[2 * D :, :], low)
    )
    s = jnp.where(core == 0, inner, got)
    per = GRP // 2
    upper = lax.rem(col, 2) == 1
    for t in range(steps - 1, -1, -1):
        s = mul_exact(s - proj[t], graw[t]) + xs[t]
        smooth[t] = jnp.where(upper, s[per:], s[:per])


VM = pl.BlockSpec(memory_space=pltpu.VMEM)


def call(kernel, outs, *args, grant=8):
    return pl.pallas_call(
        kernel,
        out_shape=tuple(jax.ShapeDtypeStruct(s, d) for s, d in outs),
        in_specs=[VM] * len(args),
        out_specs=tuple(VM for _ in outs),
        compiler_params=pltpu.CompilerParams(vmem_limit_bytes=grant << 20),
    )(*args)


def scan(transition, drive, smoother_gain, dynamics, initial_mean):
    tms, cols = lax.axis_size("tm"), lax.axis_size("col")
    steps = transition.shape[0]
    chips = tms // 2
    whole, vector = ((ALL, D), f32), ((SER, D), f32)

    def send(x, pairs):
        return lax.ppermute(
            x, ("tm", "col"), [(a * cols + b, c * cols + d) for (a, b), (c, d) in pairs]
        )

    def swap(x):
        return lax.ppermute(x, "tm", [(i, i ^ 1) for i in range(tms)])

    def turn(x, by):
        return lax.ppermute(x, "col", [(c, (c + by) % 4) for c in range(4)])

    def hop(x, moves, by=0):
        return send(
            x,
            [
                ((2 * k + h, c), (2 * (k + by) + g, d))
                for k in range(chips)
                for (c, h), (d, g) in moves
                if 0 <= k + by < chips
            ],
        )

    def shift(x, dist, lanes):
        pairs = []
        for c, h in lanes:
            by = dist if (c, h) == PRE_X else -dist
            for k in range(chips):
                if 0 <= k + by < chips:
                    pairs.append(((2 * k + h, c), (2 * (k + by) + h, c)))
        return send(x, pairs)

    def across(c):
        return [((1, h), (c, h)) for h in range(2)]

    extra = jnp.concatenate([drive, initial_mean[None]], 0)
    a_left, a_right = turn(transition, 1), turn(transition, -1)
    a_far = turn(a_left, 1)
    g_right, g_left = turn(smoother_gain, -1), turn(smoother_gain, 1)
    g_far = turn(g_right, -1)
    e_left, e_right, e_far = turn(extra, 1), turn(extra, -1), turn(extra, 2)

    quarter = (transition.shape, bf16)
    a_own, g_own, dyn = call(
        stage_kernel, [quarter, quarter, ((D, D), f32)], transition, smoother_gain, dynamics
    )
    araw, drive16, xs, proj, x_b = call(
        forward_kernel,
        [
            ((steps, D, D), bf16),
            ((steps + 1, SER, D), f32),
            ((steps, ALL, D), f32),
            ((steps, ALL, D), f32),
            whole,
        ],
        a_own, a_left, a_right, a_far,
        extra, e_left, e_right, e_far, dyn,
        grant=16,
    )
    x_bm = swap(x_b)
    graw, qy_b = call(
        backward_kernel,
        [((steps, D, D), bf16), ((ALL + D, D), f32)],
        g_own, g_left, g_right, g_far, xs, proj,
        grant=16,
    )
    qy_bm = swap(qy_b)
    own, xrow, qrow = call(chip_kernel, [whole] * 3, x_b, x_bm, qy_b, qy_bm)

    dist = 1
    while 2 * dist < chips:
        if dist > 1:
            xrow = hop(own, [(SUF_X, SUF_Y)])
            qrow = hop(own, [(SUF_Q, SUF_Y)])
        got = shift(own, dist, (SUF_X, SUF_Y, SUF_Q, PRE_X))
        own, vec = call(
            lambda *r, dist=dist: round_kernel(dist, *r),
            [whole, vector],
            own, got, xrow, qrow, araw, drive16, dyn,
        )
        dist *= 2

    got_v = shift(vec, dist, (PRE_X,))
    got = shift(own, dist, (SUF_Y,))
    xrow = hop(own, [(SUF_X, SUF_Y)])
    qrow = hop(own, [(SUF_Q, SUF_Y)])
    (leaving,) = call(mean_kernel, [vector], own, got_v)
    means = [hop(leaving, [(PRE_X, (c, 0))], 1) for c in range(4)]
    begin = means[1]
    total = (means[0] + means[1]) + (means[2] + means[3])
    means.append(hop(total, [((c, 0), (c, 1)) for c in range(4)]))
    first = lax.rem(lax.axis_index("tm"), 2) == 0
    near, mid = call(near_kernel, [vector, vector], own, xrow, begin)
    (s_one,) = call(top_kernel, [vector], near, mid, qrow, got)
    s_two = jnp.where(first, s_one, hop(s_one, [(SUF_Y, (1, 1))]))
    s_in = [hop(s_two, across(c), -1) for c in (0, 2, 1, 3)]
    part = ((steps, GRP, D), f32)
    result = ((steps, drive.shape[1], D), f32)
    xs8, proj8, mid8, filtered = call(
        mean_sweep_kernel,
        [part, part, ((GRP, D), f32), result],
        araw, drive16, dyn, x_b, x_bm, *means,
    )
    (smoothed,) = call(smooth_sweep_kernel, [result], graw, xs8, proj8, mid8, qy_bm, *s_in)
    return filtered, smoothed


def solution(mesh):
    placed = (P("tm", "col", None), P("tm", "col", None), P("tm", "col", None), P(), P("col", None))
    return jax.shard_map(
        scan,
        mesh=mesh,
        in_specs=placed,
        out_specs=(P("tm", "col", None), P("tm", "col", None)),
        check_vma=False,
    )
```

```python
import jax
import jax.numpy as jnp
from jax import lax
from jax.experimental import pallas as pl
from jax.experimental.pallas import tpu as pltpu
from jax.sharding import PartitionSpec as P


SUF_X, SUF_Y, SUF_Q = (0, 0), (1, 0), (2, 0)
PRE_X = (3, 0)
D = 256
SER = 16
GRP = 8
ALL = D + SER
f32, bf16 = jnp.float32, jnp.bfloat16


def split(x):
    hi = x.astype(bf16)
    return hi, (x - hi.astype(f32)).astype(bf16)


def dot(a, b):
    return jnp.dot(a, b, preferred_element_type=f32)


def mul_exact(x, b):
    hi, lo = split(x)
    return dot(hi, b) + dot(lo, b)


def mul(x, b):
    hi, lo = split(x)
    bhi, blo = split(b)
    return dot(hi, bhi) + (dot(lo, bhi) + dot(hi, blo))


def place():
    tm = lax.axis_index("tm")
    return tm, lax.rem(tm, 2), lax.axis_index("col")


def roles(col):
    return col == 0, col == 1, col == 3


def aligned(index, unit):
    return pl.multiple_of(index * unit, unit)


def assemble(dst, pieces, col):
    rows = pieces[0].shape[1]
    for lag, piece in zip((0, 3, 1, 2), pieces):
        dst[:, pl.ds(aligned(lax.rem(col + lag, 4), rows), rows), :] = piece[...]


def stage_kernel(a, g, dyn, a_out, g_out, dyn_out):
    a_out[...] = a[...]
    g_out[...] = g[...]
    dyn_out[...] = dyn[...]


def forward_kernel(a0, a1, a2, a3, d0, d1, d2, d3, dyn, araw, drive, xs, proj, x_out):
    tm, _, col = place()
    steps = a0.shape[0]
    assemble(araw, (a0, a1, a2, a3), col)
    per = d0.shape[1]
    for c in range(4):

        @pl.when(col == c)
        def _(c=c):
            for lag, piece in zip((0, 3, 1, 2), (d0, d1, d2, d3)):
                first = (c + lag) % 4 * per
                drive[:, first : first + per, :] = piece[...]

    start = jnp.where(tm == 0, 1.0, 0.0).astype(f32)
    dhi, dlo = split(dyn[...])
    for t in range(steps):
        if t == 0:
            xs[0, :D, :] = araw[0].astype(f32)
            xs[0, D:, :] = mul_exact(drive[steps] * start, araw[0]) + drive[0]
        else:
            new = mul_exact(xs[t - 1], araw[t])
            xs[t, :D, :] = new[:D]
            xs[t, D:, :] = new[D:] + drive[t]
        hi, lo = split(xs[t])
        proj[t] = dot(hi, dhi) + (dot(lo, dhi) + dot(hi, dlo))
    x_out[...] = xs[steps - 1]


def backward_kernel(g0, g1, g2, g3, xs, proj, graw, qy_out):
    tm, _, col = place()
    steps = g0.shape[0]
    assemble(graw, (g0, g1, g2, g3), col)

    @pl.when(tm == lax.axis_size("tm") - 1)
    def _():
        graw[steps - 1] = jnp.zeros((D, D), bf16)

    g = graw[steps - 1]
    q = g.astype(f32)
    s = mul_exact(-proj[steps - 1], g) + xs[steps - 1]
    for t in range(steps - 2, -1, -1):
        g = graw[t]
        q = mul_exact(q, g)
        s = mul_exact(s - proj[t], g) + xs[t]
    qy_out[:D, :] = q
    qy_out[D:, :] = s


def chip_kernel(x, x_m, qy, qy_m, own, xrow, qrow):
    _, core, col = place()
    suf_x, suf_y, pre_x = roles(col)

    def work(x0_ref, e0, x1, e1):
        x0, q0 = x0_ref[...], e0[:D, :]
        new = mul(x0, x1[:D, :])
        xrow[:D, :] = new[:D]
        xrow[D:, :] = new[D:] + x1[D:, :]
        qrow[:D, :] = mul(e1[:D, :], q0)
        qrow[D:, :] = jnp.zeros((SER, D), f32)
        mid = mul(x0, e1[D : 2 * D, :])
        mid = jnp.concatenate([mid[:D], mid[D:] + e1[2 * D :, :]], 0)
        new_y = e0[D:, :] + mul(mid, q0)
        rest = jnp.where(jnp.logical_or(suf_x, pre_x), xrow[...], qrow[...])
        own[...] = jnp.where(suf_y, new_y, rest)

    @pl.when(core == 0)
    def _():
        work(x, qy, x_m, qy_m)

    @pl.when(core == 1)
    def _():
        work(x_m, qy_m, x, qy)


def round_kernel(dist, own, got, xrow, qrow, kept_a, kept_d, kept_g, out, vec):
    tm, _, col = place()
    suf_x, suf_y, pre_x = roles(col)
    chip = lax.div(tm, 2)
    later = chip + dist < lax.axis_size("tm") // 2

    @pl.when(jnp.logical_not(jnp.logical_or(suf_x, suf_y)))
    def _():
        valid = jnp.where(pre_x, chip >= dist, later)
        new = mul(got[...], own[:D, :])
        out[:D, :] = jnp.where(valid, new[:D], own[:D, :])
        out[D:, :] = new[D:] + own[D:, :]

    @pl.when(suf_x)
    def _():
        new = mul(own[...], got[:D, :])
        out[:D, :] = jnp.where(later, new[:D], own[:D, :])
        out[D:, :] = jnp.where(later, new[D:] + got[D:, :], own[D:, :])

    @pl.when(suf_y)
    def _():
        mid = mul(xrow[...], got[:D, :])
        mid = jnp.concatenate([mid[:D], mid[D:] + got[D:, :]], 0)
        out[...] = own[...] + mul(mid, qrow[:D, :])

    vec[...] = out[D:, :]


def mean_kernel(own, got, out):
    out[...] = mul(got[...], own[:D, :]) + own[D:, :]


def near_kernel(own, xrow, begin, near, mid):
    x = begin[...]
    near[...] = mul(x, own[:D, :]) + own[D:, :]
    mid[...] = mul(x, xrow[:D, :]) + xrow[D:, :]


def top_kernel(near, mid, qrow, got, s_out):
    far = mul(mid[...], got[:D, :]) + got[D:, :]
    s_out[...] = near[...] + mul(far, qrow[:D, :])


def group(value, low):
    return jnp.where(low, value[:GRP], value[GRP:])


def mean_sweep(begin, araw, drive, dyn, x_b, x_bm, xs, proj, mid, filt):
    tm, core, col = place()
    steps = araw.shape[0]
    low = col < 2

    @pl.when(core == 0)
    def _():
        mid[...] = mul(begin, x_b[:D, :]) + group(x_b[D:, :], low)

    @pl.when(core == 1)
    def _():
        mid[...] = mul(begin, x_bm[:D, :]) + group(x_bm[D:, :], low)

    first = begin + jnp.where(tm == 0, 1.0, 0.0).astype(f32) * group(drive[steps], low)
    x = jnp.where(core == 0, first, mid[...])
    per = GRP // 2
    upper = lax.rem(col, 2) == 1
    for t in range(steps):
        x = mul_exact(x, araw[t]) + group(drive[t], low)
        xs[t] = x
        filt[t] = jnp.where(upper, x[per:], x[:per])
    proj[...] = mul(xs[...].reshape(steps * GRP, D), dyn[...]).reshape(steps, GRP, D)


def early():
    _, core, col = place()
    return jnp.logical_and(col == 1, core == 0)


def early_sweep_kernel(araw, drive, dyn, x_b, x_bm, m1, xs, proj, mid, filt):
    @pl.when(early())
    def _():
        begin = group(m1[...], True)
        mean_sweep(begin, araw, drive, dyn, x_b, x_bm, xs, proj, mid, filt)


def mean_sweep_kernel(
    araw, drive, dyn, x_b, x_bm, m0, m2, m3, m4, m5, xs0, proj0, mid0, filt0, xs, proj, mid, filt
):
    @pl.when(early())
    def _():
        for out, done in ((xs, xs0), (proj, proj0), (mid, mid0), (filt, filt0)):
            out[...] = done[...]

    @pl.when(jnp.logical_not(early()))
    def _():
        total = (m0[...] + m2[...]) + (m3[...] + m4[...]) + m5[...]
        begin = group(total, lax.axis_index("col") < 2)
        mean_sweep(begin, araw, drive, dyn, x_b, x_bm, xs, proj, mid, filt)


def smooth_sweep_kernel(graw, xs, proj, mid, qy_m, s0, s1, s2, s3, smooth):
    _, core, col = place()
    steps = graw.shape[0]
    low = col < 2
    got = group(s0[...] + s1[...] + (s2[...] + s3[...]), low)
    inner = mul(got, qy_m[:D, :]) + (
        mul(mid[...], qy_m[D : 2 * D, :]) + group(qy_m[2 * D :, :], low)
    )
    s = jnp.where(core == 0, inner, got)
    per = GRP // 2
    upper = lax.rem(col, 2) == 1
    for t in range(steps - 1, -1, -1):
        s = mul_exact(s - proj[t], graw[t]) + xs[t]
        smooth[t] = jnp.where(upper, s[per:], s[:per])


VM = pl.BlockSpec(memory_space=pltpu.VMEM)


def call(kernel, outs, *args, grant=8):
    return pl.pallas_call(
        kernel,
        out_shape=tuple(jax.ShapeDtypeStruct(s, d) for s, d in outs),
        in_specs=[VM] * len(args),
        out_specs=tuple(VM for _ in outs),
        compiler_params=pltpu.CompilerParams(vmem_limit_bytes=grant << 20),
    )(*args)


def scan(transition, drive, smoother_gain, dynamics, initial_mean):
    tms, cols = lax.axis_size("tm"), lax.axis_size("col")
    steps = transition.shape[0]
    chips = tms // 2
    whole, vector = ((ALL, D), f32), ((SER, D), f32)

    def send(x, pairs):
        return lax.ppermute(
            x, ("tm", "col"), [(a * cols + b, c * cols + d) for (a, b), (c, d) in pairs]
        )

    def swap(x):
        return lax.ppermute(x, "tm", [(i, i ^ 1) for i in range(tms)])

    def turn(x, by):
        return lax.ppermute(x, "col", [(c, (c + by) % 4) for c in range(4)])

    def hop(x, moves, by=0):
        return send(
            x,
            [
                ((2 * k + h, c), (2 * (k + by) + g, d))
                for k in range(chips)
                for (c, h), (d, g) in moves
                if 0 <= k + by < chips
            ],
        )

    def shift(x, dist, lanes):
        pairs = []
        for c, h in lanes:
            by = dist if (c, h) == PRE_X else -dist
            for k in range(chips):
                if 0 <= k + by < chips:
                    pairs.append(((2 * k + h, c), (2 * (k + by) + h, c)))
        return send(x, pairs)

    def across(c):
        return [((1, h), (c, h)) for h in range(2)]

    extra = jnp.concatenate([drive, initial_mean[None]], 0)
    a_left, a_right = turn(transition, 1), turn(transition, -1)
    a_far = turn(a_left, 1)
    g_right, g_left = turn(smoother_gain, -1), turn(smoother_gain, 1)
    g_far = turn(g_right, -1)
    e_left, e_right, e_far = turn(extra, 1), turn(extra, -1), turn(extra, 2)

    quarter = (transition.shape, bf16)
    a_own, g_own, dyn = call(
        stage_kernel, [quarter, quarter, ((D, D), f32)], transition, smoother_gain, dynamics
    )
    araw, drive16, xs, proj, x_b = call(
        forward_kernel,
        [
            ((steps, D, D), bf16),
            ((steps + 1, SER, D), f32),
            ((steps, ALL, D), f32),
            ((steps, ALL, D), f32),
            whole,
        ],
        a_own, a_left, a_right, a_far,
        extra, e_left, e_right, e_far, dyn,
        grant=16,
    )
    x_bm = swap(x_b)
    graw, qy_b = call(
        backward_kernel,
        [((steps, D, D), bf16), ((ALL + D, D), f32)],
        g_own, g_left, g_right, g_far, xs, proj,
        grant=16,
    )
    qy_bm = swap(qy_b)
    own, xrow, qrow = call(chip_kernel, [whole] * 3, x_b, x_bm, qy_b, qy_bm)

    dist = 1
    while 2 * dist < chips:
        if dist > 1:
            xrow = hop(own, [(SUF_X, SUF_Y)])
            qrow = hop(own, [(SUF_Q, SUF_Y)])
        got = shift(own, dist, (SUF_X, SUF_Y, SUF_Q, PRE_X))
        own, vec = call(
            lambda *r, dist=dist: round_kernel(dist, *r),
            [whole, vector],
            own, got, xrow, qrow, araw, drive16, dyn,
        )
        dist *= 2

    got_v = shift(vec, dist, (PRE_X,))
    got = shift(own, dist, (SUF_Y,))
    xrow = hop(own, [(SUF_X, SUF_Y)])
    qrow = hop(own, [(SUF_Q, SUF_Y)])
    (leaving,) = call(mean_kernel, [vector], own, got_v)
    begin = hop(leaving, [(PRE_X, SUF_Y)], 1)
    ahead = hop(leaving, [(PRE_X, PRE_X)], 1)
    means = {c: hop(ahead, [(PRE_X, (c, 0))]) for c in (0, 2)}
    means[3] = ahead
    total = means[0] + (means[2] + means[3])
    x_pass = hop(total, [((c, 0), (c, 1)) for c in (0, 2, 3)])
    x_one = hop(begin, [((1, 0), (1, 1))])
    part = ((steps, GRP, D), f32)
    result = ((steps, drive.shape[1], D), f32)
    swept = [part, part, ((GRP, D), f32), result]
    held = (araw, drive16, dyn, x_b, x_bm)
    sweep = call(early_sweep_kernel, swept, *held, begin)
    first = lax.rem(lax.axis_index("tm"), 2) == 0
    near, mid = call(near_kernel, [vector, vector], own, xrow, begin)
    (s_one,) = call(top_kernel, [vector], near, mid, qrow, got)
    s_two = jnp.where(first, s_one, hop(s_one, [(SUF_Y, (1, 1))]))
    s_in = [hop(s_two, across(c), -1) for c in (0, 2, 3, 1)]
    xs8, proj8, mid8, filtered = call(
        mean_sweep_kernel,
        swept,
        *held, means[0], means[2], means[3], x_pass, x_one, *sweep,
    )
    (smoothed,) = call(smooth_sweep_kernel, [result], graw, xs8, proj8, mid8, qy_bm, *s_in)
    return filtered, smoothed


def solution(mesh):
    placed = (P("tm", "col", None), P("tm", "col", None), P("tm", "col", None), P(), P("col", None))
    return jax.shard_map(
        scan,
        mesh=mesh,
        in_specs=placed,
        out_specs=(P("tm", "col", None), P("tm", "col", None)),
        check_vma=False,
    )
```

```python
import jax
import jax.numpy as jnp
from jax import lax
from jax.experimental import pallas as pl
from jax.experimental.pallas import tpu as pltpu
from jax.sharding import PartitionSpec as P


SUF_X, SUF_Y, SUF_Q = (0, 0), (1, 0), (2, 0)
PRE_X = (3, 0)
D = 256
SER = 16
GRP = 8
ALL = D + SER
f32, bf16 = jnp.float32, jnp.bfloat16


def split(x):
    hi = x.astype(bf16)
    return hi, (x - hi.astype(f32)).astype(bf16)


def dot(a, b):
    return jnp.dot(a, b, preferred_element_type=f32)


def mul_exact(x, b):
    hi, lo = split(x)
    return dot(hi, b) + dot(lo, b)


def mul(x, b):
    hi, lo = split(x)
    bhi, blo = split(b)
    return dot(hi, bhi) + (dot(lo, bhi) + dot(hi, blo))


def place():
    tm = lax.axis_index("tm")
    return tm, lax.rem(tm, 2), lax.axis_index("col")


def roles(col):
    return col == 0, col == 1, col == 3


def aligned(index, unit):
    return pl.multiple_of(index * unit, unit)


def assemble(dst, pieces, col):
    rows = pieces[0].shape[1]
    for lag, piece in zip((0, 3, 1, 2), pieces):
        dst[:, pl.ds(aligned(lax.rem(col + lag, 4), rows), rows), :] = piece[...]


def stage_kernel(a, g, dyn, a_out, g_out, dyn_out):
    a_out[...] = a[...]
    g_out[...] = g[...]
    dyn_out[...] = dyn[...]


def forward_kernel(a0, a1, a2, a3, d0, d1, d2, d3, dyn, araw, drive, xs, proj, x_out):
    tm, _, col = place()
    steps = a0.shape[0]
    assemble(araw, (a0, a1, a2, a3), col)
    per = d0.shape[1]
    for c in range(4):

        @pl.when(col == c)
        def _(c=c):
            for lag, piece in zip((0, 3, 1, 2), (d0, d1, d2, d3)):
                first = (c + lag) % 4 * per
                drive[:, first : first + per, :] = piece[...]

    start = jnp.where(tm == 0, 1.0, 0.0).astype(f32)
    dhi, dlo = split(dyn[...])
    for t in range(steps):
        if t == 0:
            xs[0, :D, :] = araw[0].astype(f32)
            xs[0, D:, :] = mul_exact(drive[steps] * start, araw[0]) + drive[0]
        else:
            new = mul_exact(xs[t - 1], araw[t])
            xs[t, :D, :] = new[:D]
            xs[t, D:, :] = new[D:] + drive[t]
        hi, lo = split(xs[t])
        proj[t] = dot(hi, dhi) + (dot(lo, dhi) + dot(hi, dlo))
    x_out[...] = xs[steps - 1]


def backward_kernel(g0, g1, g2, g3, xs, proj, graw, qy_out):
    tm, _, col = place()
    steps = g0.shape[0]
    assemble(graw, (g0, g1, g2, g3), col)

    @pl.when(tm == lax.axis_size("tm") - 1)
    def _():
        graw[steps - 1] = jnp.zeros((D, D), bf16)

    g = graw[steps - 1]
    q = g.astype(f32)
    s = mul_exact(-proj[steps - 1], g) + xs[steps - 1]
    for t in range(steps - 2, -1, -1):
        g = graw[t]
        q = mul_exact(q, g)
        s = mul_exact(s - proj[t], g) + xs[t]
    qy_out[:D, :] = q
    qy_out[D:, :] = s


def chip_kernel(x, x_m, qy, qy_m, own, xrow, qrow):
    _, core, col = place()
    suf_x, suf_y, pre_x = roles(col)

    def work(x0_ref, e0, x1, e1):
        x0, q0 = x0_ref[...], e0[:D, :]
        new = mul(x0, x1[:D, :])
        xrow[:D, :] = new[:D]
        xrow[D:, :] = new[D:] + x1[D:, :]
        qrow[:D, :] = mul(e1[:D, :], q0)
        qrow[D:, :] = jnp.zeros((SER, D), f32)
        mid = mul(x0, e1[D : 2 * D, :])
        mid = jnp.concatenate([mid[:D], mid[D:] + e1[2 * D :, :]], 0)
        new_y = e0[D:, :] + mul(mid, q0)
        rest = jnp.where(jnp.logical_or(suf_x, pre_x), xrow[...], qrow[...])
        own[...] = jnp.where(suf_y, new_y, rest)

    @pl.when(core == 0)
    def _():
        work(x, qy, x_m, qy_m)

    @pl.when(core == 1)
    def _():
        work(x_m, qy_m, x, qy)


def round_kernel(dist, own, got, xrow, qrow, kept_a, kept_d, kept_g, out, vec):
    tm, _, col = place()
    suf_x, suf_y, pre_x = roles(col)
    chip = lax.div(tm, 2)
    later = chip + dist < lax.axis_size("tm") // 2

    @pl.when(jnp.logical_not(jnp.logical_or(suf_x, suf_y)))
    def _():
        valid = jnp.where(pre_x, chip >= dist, later)
        new = mul(got[...], own[:D, :])
        out[:D, :] = jnp.where(valid, new[:D], own[:D, :])
        out[D:, :] = new[D:] + own[D:, :]

    @pl.when(suf_x)
    def _():
        new = mul(own[...], got[:D, :])
        out[:D, :] = jnp.where(later, new[:D], own[:D, :])
        out[D:, :] = jnp.where(later, new[D:] + got[D:, :], own[D:, :])

    @pl.when(suf_y)
    def _():
        mid = mul(xrow[...], got[:D, :])
        mid = jnp.concatenate([mid[:D], mid[D:] + got[D:, :]], 0)
        out[...] = own[...] + mul(mid, qrow[:D, :])

    vec[...] = out[D:, :]


def mean_kernel(own, got, out):
    out[...] = mul(got[...], own[:D, :]) + own[D:, :]


def near_kernel(own, xrow, begin, near, mid):
    x = begin[...]
    near[...] = mul(x, own[:D, :]) + own[D:, :]
    mid[...] = mul(x, xrow[:D, :]) + xrow[D:, :]


def top_kernel(near, mid, qrow, got, s_out):
    far = mul(mid[...], got[:D, :]) + got[D:, :]
    s_out[...] = near[...] + mul(far, qrow[:D, :])


def group(value, low):
    return jnp.where(low, value[:GRP], value[GRP:])


def mean_sweep(begin, araw, drive, dyn, x_b, x_bm, xs, proj, mid, filt):
    tm, core, col = place()
    steps = araw.shape[0]
    low = col < 2

    @pl.when(core == 0)
    def _():
        mid[...] = mul(begin, x_b[:D, :]) + group(x_b[D:, :], low)

    @pl.when(core == 1)
    def _():
        mid[...] = mul(begin, x_bm[:D, :]) + group(x_bm[D:, :], low)

    first = begin + jnp.where(tm == 0, 1.0, 0.0).astype(f32) * group(drive[steps], low)
    x = jnp.where(core == 0, first, mid[...])
    per = GRP // 2
    upper = lax.rem(col, 2) == 1
    for t in range(steps):
        x = mul_exact(x, araw[t]) + group(drive[t], low)
        xs[t] = x
        filt[t] = jnp.where(upper, x[per:], x[:per])
    proj[...] = mul(xs[...].reshape(steps * GRP, D), dyn[...]).reshape(steps, GRP, D)


def early():
    _, core, col = place()
    return jnp.logical_and(col == 1, core == 0)


def early_sweep_kernel(araw, drive, dyn, x_b, x_bm, m1, xs, proj, mid, filt):
    @pl.when(early())
    def _():
        begin = group(m1[...], True)
        mean_sweep(begin, araw, drive, dyn, x_b, x_bm, xs, proj, mid, filt)


def mean_sweep_kernel(
    araw, drive, dyn, x_b, x_bm, m0, m2, m3, m4, m5, xs0, proj0, mid0, filt0, xs, proj, mid, filt
):
    @pl.when(early())
    def _():
        for out, done in ((xs, xs0), (proj, proj0), (mid, mid0), (filt, filt0)):
            out[...] = done[...]

    @pl.when(jnp.logical_not(early()))
    def _():
        total = (m0[...] + m2[...]) + (m3[...] + m4[...]) + m5[...]
        begin = group(total, lax.axis_index("col") < 2)
        mean_sweep(begin, araw, drive, dyn, x_b, x_bm, xs, proj, mid, filt)


def smooth_sweep_kernel(graw, xs, proj, mid, qy_m, s0, s1, s2, s3, smooth):
    _, core, col = place()
    steps = graw.shape[0]
    low = col < 2
    got = group(s0[...] + s1[...] + (s2[...] + s3[...]), low)
    inner = mul(got, qy_m[:D, :]) + (
        mul(mid[...], qy_m[D : 2 * D, :]) + group(qy_m[2 * D :, :], low)
    )
    s = jnp.where(core == 0, inner, got)
    per = GRP // 2
    upper = lax.rem(col, 2) == 1
    for t in range(steps - 1, -1, -1):
        s = mul_exact(s - proj[t], graw[t]) + xs[t]
        smooth[t] = jnp.where(upper, s[per:], s[:per])


VM = pl.BlockSpec(memory_space=pltpu.VMEM)


def call(kernel, outs, *args, grant=8):
    return pl.pallas_call(
        kernel,
        out_shape=tuple(jax.ShapeDtypeStruct(s, d) for s, d in outs),
        in_specs=[VM] * len(args),
        out_specs=tuple(VM for _ in outs),
        compiler_params=pltpu.CompilerParams(vmem_limit_bytes=grant << 20),
    )(*args)


def scan(transition, drive, smoother_gain, dynamics, initial_mean):
    tms, cols = lax.axis_size("tm"), lax.axis_size("col")
    steps = transition.shape[0]
    chips = tms // 2
    whole, vector = ((ALL, D), f32), ((SER, D), f32)

    def send(x, pairs):
        return lax.ppermute(
            x, ("tm", "col"), [(a * cols + b, c * cols + d) for (a, b), (c, d) in pairs]
        )

    def swap(x):
        return lax.ppermute(x, "tm", [(i, i ^ 1) for i in range(tms)])

    def turn(x, by):
        return lax.ppermute(x, "col", [(c, (c + by) % 4) for c in range(4)])

    def hop(x, moves, by=0):
        return send(
            x,
            [
                ((2 * k + h, c), (2 * (k + by) + g, d))
                for k in range(chips)
                for (c, h), (d, g) in moves
                if 0 <= k + by < chips
            ],
        )

    def shift(x, dist, lanes):
        pairs = []
        for c, h in lanes:
            by = dist if (c, h) == PRE_X else -dist
            for k in range(chips):
                if 0 <= k + by < chips:
                    pairs.append(((2 * k + h, c), (2 * (k + by) + h, c)))
        return send(x, pairs)

    def across(c):
        return [((1, h), (c, h)) for h in range(2)]

    extra = jnp.concatenate([drive, initial_mean[None]], 0)
    a_left, a_right = turn(transition, 1), turn(transition, -1)
    a_far = turn(a_left, 1)
    g_right, g_left = turn(smoother_gain, -1), turn(smoother_gain, 1)
    g_far = turn(g_right, -1)
    e_left, e_right, e_far = turn(extra, 1), turn(extra, -1), turn(extra, 2)

    quarter = (transition.shape, bf16)
    a_own, g_own, dyn = call(
        stage_kernel, [quarter, quarter, ((D, D), f32)], transition, smoother_gain, dynamics
    )
    araw, drive16, xs, proj, x_b = call(
        forward_kernel,
        [
            ((steps, D, D), bf16),
            ((steps + 1, SER, D), f32),
            ((steps, ALL, D), f32),
            ((steps, ALL, D), f32),
            whole,
        ],
        a_own, a_left, a_right, a_far,
        extra, e_left, e_right, e_far, dyn,
        grant=16,
    )
    x_bm = swap(x_b)
    graw, qy_b = call(
        backward_kernel,
        [((steps, D, D), bf16), ((ALL + D, D), f32)],
        g_own, g_left, g_right, g_far, xs, proj,
        grant=16,
    )
    qy_bm = swap(qy_b)
    own, xrow, qrow = call(chip_kernel, [whole] * 3, x_b, x_bm, qy_b, qy_bm)

    dist = 1
    while 2 * dist < chips:
        if dist > 1:
            xrow = hop(own, [(SUF_X, SUF_Y)])
            qrow = hop(own, [(SUF_Q, SUF_Y)])
        got = shift(own, dist, (SUF_X, SUF_Y, SUF_Q, PRE_X))
        own, vec = call(
            lambda *r, dist=dist: round_kernel(dist, *r),
            [whole, vector],
            own, got, xrow, qrow, araw, drive16, dyn,
        )
        dist *= 2

    got_v = shift(vec, dist, (PRE_X,))
    got = shift(own, dist, (SUF_Y,))
    xrow = hop(own, [(SUF_X, SUF_Y)])
    qrow = hop(own, [(SUF_Q, SUF_Y)])
    (leaving,) = call(mean_kernel, [vector], own, got_v)
    begin = hop(leaving, [(PRE_X, SUF_Y)], 1)
    means = {3: hop(leaving, [(PRE_X, PRE_X)], 1)}
    for c in (0, 2):
        means[c] = hop(begin, [(SUF_Y, (c, 0))])
    total = means[0] + (means[2] + means[3])
    x_pass = hop(total, [((c, 0), (c, 1)) for c in (0, 2, 3)])
    x_one = hop(begin, [((1, 0), (1, 1))])
    part = ((steps, GRP, D), f32)
    result = ((steps, drive.shape[1], D), f32)
    swept = [part, part, ((GRP, D), f32), result]
    held = (araw, drive16, dyn, x_b, x_bm)
    ahead = call(early_sweep_kernel, swept, *held, begin)
    first = lax.rem(lax.axis_index("tm"), 2) == 0
    near, mid = call(near_kernel, [vector, vector], own, xrow, begin)
    (s_one,) = call(top_kernel, [vector], near, mid, qrow, got)
    s_two = jnp.where(first, s_one, hop(s_one, [(SUF_Y, (1, 1))]))
    s_in = [hop(s_two, across(c), -1) for c in (0, 2, 1, 3)]
    xs8, proj8, mid8, filtered = call(
        mean_sweep_kernel,
        swept,
        *held, means[0], means[2], means[3], x_pass, x_one, *ahead,
    )
    (smoothed,) = call(smooth_sweep_kernel, [result], graw, xs8, proj8, mid8, qy_bm, *s_in)
    return filtered, smoothed


def solution(mesh):
    placed = (P("tm", "col", None), P("tm", "col", None), P("tm", "col", None), P(), P("col", None))
    return jax.shard_map(
        scan,
        mesh=mesh,
        in_specs=placed,
        out_specs=(P("tm", "col", None), P("tm", "col", None)),
        check_vma=False,
    )
```

```python
import jax
import jax.numpy as jnp
from jax import lax
from jax.experimental import pallas as pl
from jax.experimental.pallas import tpu as pltpu
from jax.sharding import PartitionSpec as P


SUF_X, SUF_Y, SUF_Q = (0, 0), (1, 0), (2, 0)
PRE_X = (3, 0)
D = 256
SER = 16
GRP = 8
ALL = D + SER
f32, bf16 = jnp.float32, jnp.bfloat16


def split(x):
    hi = x.astype(bf16)
    return hi, (x - hi.astype(f32)).astype(bf16)


def dot(a, b):
    return jnp.dot(a, b, preferred_element_type=f32)


def mul_exact(x, b):
    hi, lo = split(x)
    return dot(hi, b) + dot(lo, b)


def mul(x, b):
    hi, lo = split(x)
    bhi, blo = split(b)
    return dot(hi, bhi) + (dot(lo, bhi) + dot(hi, blo))


def place():
    tm = lax.axis_index("tm")
    return tm, lax.rem(tm, 2), lax.axis_index("col")


def roles(col):
    return col == 0, col == 1, col == 3


def aligned(index, unit):
    return pl.multiple_of(index * unit, unit)


def assemble(dst, pieces, col):
    rows = pieces[0].shape[1]
    for lag, piece in zip((0, 3, 1, 2), pieces):
        dst[:, pl.ds(aligned(lax.rem(col + lag, 4), rows), rows), :] = piece[...]


def stage_kernel(a, g, dyn, a_out, g_out, dyn_out):
    a_out[...] = a[...]
    g_out[...] = g[...]
    dyn_out[...] = dyn[...]


def forward_kernel(a0, a1, a2, a3, d0, d1, d2, d3, dyn, araw, drive, xs, proj, x_out):
    tm, _, col = place()
    steps = a0.shape[0]
    assemble(araw, (a0, a1, a2, a3), col)
    per = d0.shape[1]
    for c in range(4):

        @pl.when(col == c)
        def _(c=c):
            for lag, piece in zip((0, 3, 1, 2), (d0, d1, d2, d3)):
                first = (c + lag) % 4 * per
                drive[:, first : first + per, :] = piece[...]

    start = jnp.where(tm == 0, 1.0, 0.0).astype(f32)
    dhi, dlo = split(dyn[...])
    for t in range(steps):
        if t == 0:
            xs[0, :D, :] = araw[0].astype(f32)
            xs[0, D:, :] = mul_exact(drive[steps] * start, araw[0]) + drive[0]
        else:
            new = mul_exact(xs[t - 1], araw[t])
            xs[t, :D, :] = new[:D]
            xs[t, D:, :] = new[D:] + drive[t]
        hi, lo = split(xs[t])
        proj[t] = dot(hi, dhi) + (dot(lo, dhi) + dot(hi, dlo))
    x_out[...] = xs[steps - 1]


def backward_kernel(g0, g1, g2, g3, xs, proj, graw, qy_out):
    tm, _, col = place()
    steps = g0.shape[0]
    assemble(graw, (g0, g1, g2, g3), col)

    @pl.when(tm == lax.axis_size("tm") - 1)
    def _():
        graw[steps - 1] = jnp.zeros((D, D), bf16)

    g = graw[steps - 1]
    q = g.astype(f32)
    s = mul_exact(-proj[steps - 1], g) + xs[steps - 1]
    for t in range(steps - 2, -1, -1):
        g = graw[t]
        q = mul_exact(q, g)
        s = mul_exact(s - proj[t], g) + xs[t]
    qy_out[:D, :] = q
    qy_out[D:, :] = s


def chip_kernel(x, x_m, qy, qy_m, own, xrow, qrow):
    _, core, col = place()
    suf_x, suf_y, pre_x = roles(col)

    def work(x0_ref, e0, x1, e1):
        x0, q0 = x0_ref[...], e0[:D, :]
        new = mul(x0, x1[:D, :])
        xrow[:D, :] = new[:D]
        xrow[D:, :] = new[D:] + x1[D:, :]
        qrow[:D, :] = mul(e1[:D, :], q0)
        qrow[D:, :] = jnp.zeros((SER, D), f32)
        mid = mul(x0, e1[D : 2 * D, :])
        mid = jnp.concatenate([mid[:D], mid[D:] + e1[2 * D :, :]], 0)
        new_y = e0[D:, :] + mul(mid, q0)
        rest = jnp.where(jnp.logical_or(suf_x, pre_x), xrow[...], qrow[...])
        own[...] = jnp.where(suf_y, new_y, rest)

    @pl.when(core == 0)
    def _():
        work(x, qy, x_m, qy_m)

    @pl.when(core == 1)
    def _():
        work(x_m, qy_m, x, qy)


def round_kernel(dist, own, got, xrow, qrow, kept_a, kept_d, kept_g, out, vec):
    tm, _, col = place()
    suf_x, suf_y, pre_x = roles(col)
    chip = lax.div(tm, 2)
    later = chip + dist < lax.axis_size("tm") // 2

    @pl.when(jnp.logical_not(jnp.logical_or(suf_x, suf_y)))
    def _():
        valid = jnp.where(pre_x, chip >= dist, later)
        new = mul(got[...], own[:D, :])
        out[:D, :] = jnp.where(valid, new[:D], own[:D, :])
        out[D:, :] = new[D:] + own[D:, :]

    @pl.when(suf_x)
    def _():
        new = mul(own[...], got[:D, :])
        out[:D, :] = jnp.where(later, new[:D], own[:D, :])
        out[D:, :] = jnp.where(later, new[D:] + got[D:, :], own[D:, :])

    @pl.when(suf_y)
    def _():
        mid = mul(xrow[...], got[:D, :])
        mid = jnp.concatenate([mid[:D], mid[D:] + got[D:, :]], 0)
        out[...] = own[...] + mul(mid, qrow[:D, :])

    vec[...] = out[D:, :]


def mean_kernel(own, got, out):
    out[...] = mul(got[...], own[:D, :]) + own[D:, :]


def near_kernel(own, xrow, begin, near, mid):
    x = begin[...]
    near[...] = mul(x, own[:D, :]) + own[D:, :]
    mid[...] = mul(x, xrow[:D, :]) + xrow[D:, :]


def top_kernel(near, mid, qrow, got, s_out):
    far = mul(mid[...], got[:D, :]) + got[D:, :]
    s_out[...] = near[...] + mul(far, qrow[:D, :])


def group(value, low):
    return jnp.where(low, value[:GRP], value[GRP:])


def mean_sweep(begin, araw, drive, dyn, x_b, x_bm, xs, proj, mid, filt):
    tm, core, col = place()
    steps = araw.shape[0]
    low = col < 2

    @pl.when(core == 0)
    def _():
        mid[...] = mul(begin, x_b[:D, :]) + group(x_b[D:, :], low)

    @pl.when(core == 1)
    def _():
        mid[...] = mul(begin, x_bm[:D, :]) + group(x_bm[D:, :], low)

    first = begin + jnp.where(tm == 0, 1.0, 0.0).astype(f32) * group(drive[steps], low)
    x = jnp.where(core == 0, first, mid[...])
    per = GRP // 2
    upper = lax.rem(col, 2) == 1
    for t in range(steps):
        x = mul_exact(x, araw[t]) + group(drive[t], low)
        xs[t] = x
        filt[t] = jnp.where(upper, x[per:], x[:per])
    proj[...] = mul(xs[...].reshape(steps * GRP, D), dyn[...]).reshape(steps, GRP, D)


def early():
    _, core, col = place()
    return jnp.logical_and(col == 1, core == 0)


def early_sweep_kernel(araw, drive, dyn, x_b, x_bm, m1, xs, proj, mid, filt):
    @pl.when(early())
    def _():
        begin = group(m1[...], True)
        mean_sweep(begin, araw, drive, dyn, x_b, x_bm, xs, proj, mid, filt)


def mean_sweep_kernel(
    araw, drive, dyn, x_b, x_bm, m0, m2, m3, m4, m5, xs0, proj0, mid0, filt0, xs, proj, mid, filt
):
    @pl.when(early())
    def _():
        for out, done in ((xs, xs0), (proj, proj0), (mid, mid0), (filt, filt0)):
            out[...] = done[...]

    @pl.when(jnp.logical_not(early()))
    def _():
        total = (m0[...] + m2[...]) + (m3[...] + m4[...]) + m5[...]
        begin = group(total, lax.axis_index("col") < 2)
        mean_sweep(begin, araw, drive, dyn, x_b, x_bm, xs, proj, mid, filt)


def smooth_sweep_kernel(graw, xs, proj, mid, qy_m, s0, s1, s2, s3, smooth):
    _, core, col = place()
    steps = graw.shape[0]
    low = col < 2
    got = group(s0[...] + s1[...] + (s2[...] + s3[...]), low)
    inner = mul(got, qy_m[:D, :]) + (
        mul(mid[...], qy_m[D : 2 * D, :]) + group(qy_m[2 * D :, :], low)
    )
    s = jnp.where(core == 0, inner, got)
    per = GRP // 2
    upper = lax.rem(col, 2) == 1
    for t in range(steps - 1, -1, -1):
        s = mul_exact(s - proj[t], graw[t]) + xs[t]
        smooth[t] = jnp.where(upper, s[per:], s[:per])


VM = pl.BlockSpec(memory_space=pltpu.VMEM)


def call(kernel, outs, *args, grant=8):
    return pl.pallas_call(
        kernel,
        out_shape=tuple(jax.ShapeDtypeStruct(s, d) for s, d in outs),
        in_specs=[VM] * len(args),
        out_specs=tuple(VM for _ in outs),
        compiler_params=pltpu.CompilerParams(vmem_limit_bytes=grant << 20),
    )(*args)


def scan(transition, drive, smoother_gain, dynamics, initial_mean):
    tms, cols = lax.axis_size("tm"), lax.axis_size("col")
    steps = transition.shape[0]
    chips = tms // 2
    whole, vector = ((ALL, D), f32), ((SER, D), f32)

    def send(x, pairs):
        return lax.ppermute(
            x, ("tm", "col"), [(a * cols + b, c * cols + d) for (a, b), (c, d) in pairs]
        )

    def swap(x):
        return lax.ppermute(x, "tm", [(i, i ^ 1) for i in range(tms)])

    def turn(x, by):
        return lax.ppermute(x, "col", [(c, (c + by) % 4) for c in range(4)])

    def hop(x, moves, by=0):
        return send(
            x,
            [
                ((2 * k + h, c), (2 * (k + by) + g, d))
                for k in range(chips)
                for (c, h), (d, g) in moves
                if 0 <= k + by < chips
            ],
        )

    def shift(x, dist, lanes):
        pairs = []
        for c, h in lanes:
            by = dist if (c, h) == PRE_X else -dist
            for k in range(chips):
                if 0 <= k + by < chips:
                    pairs.append(((2 * k + h, c), (2 * (k + by) + h, c)))
        return send(x, pairs)

    def across(c):
        return [((1, h), (c, h)) for h in range(2)]

    extra = jnp.concatenate([drive, initial_mean[None]], 0)
    a_left, a_right = turn(transition, 1), turn(transition, -1)
    a_far = turn(a_left, 1)
    g_right, g_left = turn(smoother_gain, -1), turn(smoother_gain, 1)
    g_far = turn(g_right, -1)
    e_left, e_right, e_far = turn(extra, 1), turn(extra, -1), turn(extra, 2)

    quarter = (transition.shape, bf16)
    a_own, g_own, dyn = call(
        stage_kernel, [quarter, quarter, ((D, D), f32)], transition, smoother_gain, dynamics
    )
    araw, drive16, xs, proj, x_b = call(
        forward_kernel,
        [
            ((steps, D, D), bf16),
            ((steps + 1, SER, D), f32),
            ((steps, ALL, D), f32),
            ((steps, ALL, D), f32),
            whole,
        ],
        a_own, a_left, a_right, a_far,
        extra, e_left, e_right, e_far, dyn,
        grant=16,
    )
    x_bm = swap(x_b)
    graw, qy_b = call(
        backward_kernel,
        [((steps, D, D), bf16), ((ALL + D, D), f32)],
        g_own, g_left, g_right, g_far, xs, proj,
        grant=16,
    )
    qy_bm = swap(qy_b)
    own, xrow, qrow = call(chip_kernel, [whole] * 3, x_b, x_bm, qy_b, qy_bm)

    dist = 1
    while 2 * dist < chips:
        if dist > 1:
            xrow = hop(own, [(SUF_X, SUF_Y)])
            qrow = hop(own, [(SUF_Q, SUF_Y)])
        got = shift(own, dist, (SUF_X, SUF_Y, SUF_Q, PRE_X))
        own, vec = call(
            lambda *r, dist=dist: round_kernel(dist, *r),
            [whole, vector],
            own, got, xrow, qrow, araw, drive16, dyn,
        )
        dist *= 2

    got_v = shift(vec, dist, (PRE_X,))
    got = shift(own, dist, (SUF_Y,))
    xrow = hop(own, [(SUF_X, SUF_Y)])
    qrow = hop(own, [(SUF_Q, SUF_Y)])
    (leaving,) = call(mean_kernel, [vector], own, got_v)
    means = [hop(leaving, [(PRE_X, (c, 0))], 1) for c in range(4)]
    begin = means[1]
    total = means[0] + (means[2] + means[3])
    x_pass = hop(total, [((c, 0), (c, 1)) for c in (0, 2, 3)])
    x_one = hop(begin, [((1, 0), (1, 1))])
    part = ((steps, GRP, D), f32)
    result = ((steps, drive.shape[1], D), f32)
    swept = [part, part, ((GRP, D), f32), result]
    held = (araw, drive16, dyn, x_b, x_bm)
    ahead = call(early_sweep_kernel, swept, *held, begin)
    first = lax.rem(lax.axis_index("tm"), 2) == 0
    near, mid = call(near_kernel, [vector, vector], own, xrow, begin)
    (s_one,) = call(top_kernel, [vector], near, mid, qrow, got)
    s_two = jnp.where(first, s_one, hop(s_one, [(SUF_Y, (1, 1))]))
    s_in = [hop(s_two, across(c), -1) for c in (0, 2, 1, 3)]
    xs8, proj8, mid8, filtered = call(
        mean_sweep_kernel,
        swept,
        *held, means[0], means[2], means[3], x_pass, x_one, *ahead,
    )
    (smoothed,) = call(smooth_sweep_kernel, [result], graw, xs8, proj8, mid8, qy_bm, *s_in)
    return filtered, smoothed


def solution(mesh):
    placed = (P("tm", "col", None), P("tm", "col", None), P("tm", "col", None), P(), P("col", None))
    return jax.shard_map(
        scan,
        mesh=mesh,
        in_specs=placed,
        out_specs=(P("tm", "col", None), P("tm", "col", None)),
        check_vma=False,
    )
```
